256 devices in a mesh: tower: 4 (over y), dp: 64 (over z, x, core).
Axes of the slice: x: 4, y: 4, z: 8, core: 2. Of those that a mesh axis runs over, the one named last changes fastest.
Arguments:
- query_hidden: bfloat16 [12288, 2304], P('dp'), may hold values from -6 to 6
- passage_hidden: bfloat16 [12288, 3072], P(('tower', 'dp')), may hold values from -6 to 6
- pool_hidden: bfloat16 [131072, 3072], P(('tower', 'dp')), may hold values from -6 to 6
- query_proj: bfloat16 [2304, 768], replicated, may hold values from -0.125 to 0.125
- passage_proj: bfloat16 [3072, 768], replicated, may hold values from -0.109375 to 0.109375
- negative_ids: int32 [12288, 8], P('dp'), may hold values from 0 to 131071, as said below
Outputs:
- query_grad: bfloat16 [12288, 768], P(('dp', 'tower'))
- passage_grad: bfloat16 [12288, 768], P(('tower', 'dp'))
- negative_grad: bfloat16 [131072, 768], P(('tower', 'dp'))
The draws below stay inside these ranges and needn't reach their ends.
Inputs may be any that keep to these rules, and one draw needn't show every extreme that they name: `negative_ids`: the owner of pool row r is the device with index r // 512 along tower+dp. Among the 1536 ids of one index of dp, at most 12 have one owner, and in every draw some owner gets exactly 12 of them; ids may repeat.
All inputs are finite; a program needn't handle non-finite values.
Results may differ from the reference program's by a relative error of at most 0.015.
Values may be sent and summed in bfloat16 or wider, within the bound.
A program may use at most 128 MiB of HBM per device.

```python
import jax
import jax.numpy as jnp
from jax import lax

D_QUERY = 2304
D_PASSAGE = 3072
EMB = 768
NEG = 8
Q_DEV = 192
POOL_DEV = 512
QUERIES = 12288
POOL = 131072
CAP = 12
N_TOWER = 4
N_DP = 64


def draw_negative_ids(key, part):
    owner_total = N_TOWER * N_DP
    slot_total = owner_total * CAP
    entry_total = Q_DEV * NEG

    def receiver_ids(receiver):
        folded = jax.random.fold_in(jax.random.fold_in(key, 7321), receiver)
        split_keys = jax.random.split(folded, 4)
        chosen = jax.random.randint(split_keys[0], (), 0, owner_total)
        places = jnp.arange(slot_total, dtype=jnp.int32)
        slot_owner = places // CAP
        jitter = jax.random.randint(split_keys[1], (slot_total,), 0, 65536)
        ranking = jnp.where(slot_owner == chosen, places, (jitter + 1) * slot_total + places)
        ordering = jnp.argsort(ranking, stable=True)[:entry_total]
        picked = slot_owner[ordering]
        picked = picked[jax.random.permutation(split_keys[2], entry_total)]
        pool_rows = jax.random.randint(split_keys[3], (entry_total,), 0, POOL_DEV)
        return (picked * POOL_DEV + pool_rows).astype(jnp.int32).reshape(Q_DEV, NEG)
    all_ids = jax.vmap(receiver_ids)(jnp.arange(N_DP, dtype=jnp.int32))
    return all_ids.reshape(Q_DEV * N_DP, NEG)


def level_of(rng, dims, cuts, least, largest):
    gain, own = 1.0, jax.random.fold_in(rng, 6)
    for axis_at, parts in cuts:
        steps = jnp.exp(jax.random.uniform(jax.random.fold_in(own, axis_at), (parts,), jnp.float32, least / len(cuts), largest / len(cuts)))
        gain = gain * jnp.repeat(steps, dims[axis_at] // parts).reshape([-1 if axis == axis_at else 1 for axis in range(len(dims))])
    return gain


def scatter_about(key, dims, scale, limit, cuts=(), kind=jnp.bfloat16):
    drawn = scale * jax.random.normal(key, dims, jnp.float32)
    if cuts:
        drawn = drawn * level_of(key, dims, cuts, -0.22, 0.18)
    return jnp.clip(drawn, -limit, limit).astype(kind)


def setup_inputs(seed: int = 0) -> dict:
    seeds = jax.random.split(jax.random.key(seed), 7)
    return {
        "query_hidden": scatter_about(seeds[0], (QUERIES, D_QUERY), 1.0, 6.0, ((0, 64),)),
        "passage_hidden": scatter_about(seeds[1], (QUERIES, D_PASSAGE), 1.0, 6.0, ((0, 256),)),
        "pool_hidden": scatter_about(seeds[2], (POOL, D_PASSAGE), 1.0, 6.0, ((0, 256),)),
        "query_proj": scatter_about(seeds[3], (D_QUERY, EMB), D_QUERY ** -0.5, 0.125),
        "passage_proj": scatter_about(seeds[4], (D_PASSAGE, EMB), D_PASSAGE ** -0.5, 0.109375),
        "negative_ids": draw_negative_ids(jax.random.fold_in(seeds[6], 71), 0),
    }


logit_scale = 50.0

def unit_rows(hidden, weight):
    projected = jnp.dot(hidden, weight, preferred_element_type=jnp.float32)
    length = jnp.sqrt(lax.optimization_barrier(jnp.sum(projected * projected, axis=1, keepdims=True)) + 1e-06)
    return (projected / length).astype(jnp.bfloat16)

def reference(query_hidden, passage_hidden, pool_hidden, query_proj, passage_proj, negative_ids):
    query_unit = unit_rows(query_hidden, query_proj)
    passage_unit = unit_rows(passage_hidden, passage_proj)
    pool_unit = unit_rows(pool_hidden, passage_proj)
    emb_width = query_unit.shape[1]
    query_blocks = query_unit.reshape(N_DP, Q_DEV, emb_width)
    id_blocks = negative_ids.reshape(N_DP, Q_DEV, NEG)

    def score_block(totals, inputs):
        passage_acc, pool_acc = totals
        block_index, queries, named_ids = inputs
        first_row = (block_index * Q_DEV).astype(jnp.int32)
        scores = logit_scale * lax.dot_general(queries, passage_unit, (((1,), (1,)), ((), ())), preferred_element_type=jnp.float32)
        exp_scores = jnp.exp(scores)
        weights = (exp_scores / lax.optimization_barrier(jnp.sum(exp_scores, axis=1, keepdims=True))).astype(jnp.bfloat16)
        positives = lax.dynamic_slice_in_dim(passage_unit, first_row, Q_DEV, 0)
        query_wide = queries.astype(jnp.float32)
        pos_score = logit_scale * lax.optimization_barrier(jnp.sum(query_wide * positives.astype(jnp.float32), axis=1))
        fetched = pool_unit[named_ids]
        fetched_wide = fetched.astype(jnp.float32)
        neg_score = logit_scale * jnp.einsum('qe,qke->qk', query_wide, fetched_wide)
        pos_exp = jnp.exp(pos_score)
        neg_exp = jnp.exp(neg_score)
        hard_total = pos_exp + lax.optimization_barrier(jnp.sum(neg_exp, axis=1))
        pos_weight = pos_exp / hard_total
        hard_weight = neg_exp / hard_total[:, None]
        query_grad = logit_scale * (jnp.dot(weights, passage_unit, preferred_element_type=jnp.float32) + (pos_weight - 2.0)[:, None] * positives.astype(jnp.float32) + jnp.einsum('qk,qke->qe', hard_weight, fetched_wide))
        batch_term = lax.dot_general(weights, queries, (((0,), (0,)), ((), ())), preferred_element_type=jnp.float32)
        passage_acc = passage_acc + logit_scale * batch_term
        own_part = lax.dynamic_slice_in_dim(passage_acc, first_row, Q_DEV, 0)
        own_part = own_part + logit_scale * (pos_weight - 2.0)[:, None] * query_wide
        passage_acc = lax.dynamic_update_slice_in_dim(passage_acc, own_part, first_row, 0)
        entry_grad = (logit_scale * hard_weight[:, :, None] * query_wide[:, None, :]).reshape(Q_DEV * NEG, emb_width)
        pool_acc = pool_acc.at[named_ids.reshape(-1)].add(entry_grad)
        return ((passage_acc, pool_acc), query_grad.astype(jnp.bfloat16))
    start_totals = (jnp.zeros((Q_DEV * N_DP, emb_width), jnp.float32), jnp.zeros((pool_unit.shape[0], emb_width), jnp.float32))
    block_ids = jnp.arange(N_DP, dtype=jnp.int32)
    (passage_acc, pool_acc), query_grads = lax.scan(score_block, start_totals, (block_ids, query_blocks, id_blocks))
    return (query_grads.reshape(Q_DEV * N_DP, emb_width), passage_acc.astype(jnp.bfloat16), pool_acc.astype(jnp.bfloat16))
```

```python
import functools

import jax
import jax.numpy as jnp
from jax import lax
from jax.experimental import pallas as pl
from jax.experimental.pallas import tpu as pltpu
from jax.sharding import PartitionSpec as P

logit_scale = 50.0
MESH = pl.DeviceIdType.MESH
NY, NZ, NX, NC = 4, 8, 4, 2
PLANE = NY * NX * NC
F32 = jnp.float32
BF16 = jnp.bfloat16


def place():
    y = lax.axis_index("tower")
    dp = lax.axis_index("dp")
    return y, dp, dp // 8, (dp // 2) % 4, dp % 2


class Route:
    def __init__(self, count, dest, source, slot, own, item=None):
        self.count, self.dest, self.source = count, dest, source
        self.slot, self.own, self.item = slot, own, item


def routes():
    y, dp, z, x, c = place()
    line = x * 2 + c
    member, chip, core_line = y * 8 + line, y * 4 + x, z * 2 + c
    sibling = dp + 1 - 2 * c
    lead = (z % 2) * 4 + y
    at_home = z // 2 == y

    def around(base, i, n):
        return lax.rem(base + i, n)

    def plane(i):
        m = around(member, i, 32)
        return m // 8, z * 8 + m % 8

    def plane_core(i):
        n = around(chip, i, 16)
        return n // 4, z * 8 + (n % 4) * 2 + c

    def zcore(i):
        g = around(core_line, i, 16)
        return y, (g // 2) * 8 + x * 2 + g % 2

    def holder(i):
        return z // 2, around(z, i, 8) * 8 + line

    def home(i):
        k = around(lead, i, 8)
        return k % 4, (2 * y + k // 4) * 8 + line

    perm_e = (dp % 4, y * 16 + dp // 4)
    perm_f = (dp // 16, (dp % 16) * 4 + y)
    perm_own = (dp % 4 == y) & (y * 16 + dp // 4 == dp)
    perm_f_own = (dp // 16 == y) & ((dp % 16) * 4 + y == dp)
    return {
        "plane": Route(32, plane, plane, member, "yes", lambda i: around(member, i, 32)),
        "plane_core": Route(16, plane_core, plane_core, chip, "yes", lambda i: around(chip, i, 16)),
        "zline": Route(8, lambda i: (y, around(z, i, 8) * 8 + line), lambda i: (y, around(z, i, 8) * 8 + line), z, "yes"),
        "zcore": Route(16, zcore, zcore, core_line, "yes"),
        "holder": Route(8, holder, home, lead, at_home),
        "home": Route(8, home, holder, z, at_home, lambda i: around(lead, i, 8)),
        "sibling": Route(1, lambda i: (y, sibling), lambda i: (y, sibling), 0, None),
        "to_query": Route(1, lambda i: perm_e, lambda i: perm_f, 0, perm_own),
        "to_passage": Route(1, lambda i: perm_f, lambda i: perm_e, 0, perm_f_own),
    }


def loop(lo, hi, body):
    def step(i, carry):
        body(i)
        return carry

    lax.fori_loop(lo, hi, step, 0)


def enter(names, table):
    barrier = pltpu.get_barrier_semaphore()
    wanted = 0
    for name in names:
        route = table[name]

        def greet(i, route=route):
            ty, td = route.source(i)
            pl.semaphore_signal(barrier, inc=1, device_id=(ty, td), device_id_type=MESH)

        if route.own is None:
            greet(0)
            wanted = wanted + 1
            continue
        if route.own == "yes" if isinstance(route.own, str) else False:
            loop(1, route.count, greet)
            wanted = wanted + route.count - 1
            continue

        @pl.when(jnp.logical_not(route.own))
        def _(greet=greet):
            greet(0)

        if route.count > 1:
            loop(1, route.count, greet)
        wanted = wanted + route.count - 1 + jnp.where(route.own, 0, 1)
    pl.semaphore_wait(barrier, wanted)


class Transfer:
    def __init__(self, route, src, dst, send_sem, recv_sem):
        self.route, self.src, self.dst = route, src, dst
        self.send_sem, self.recv_sem = send_sem, recv_sem

    def copy(self, i):
        ty, td = self.route.dest(i)
        slot = self.route.slot
        return pltpu.make_async_remote_copy(
            src_ref=self.src(i),
            dst_ref=self.dst(slot),
            send_sem=self.send_sem.at[i],
            recv_sem=self.recv_sem.at[slot],
            device_id=(ty, td),
            device_id_type=MESH,
        )

    def local(self):
        slot = self.route.slot
        return pltpu.make_async_copy(self.src(0), self.dst(slot), self.recv_sem.at[slot])

    def each(self, far, near):
        own = self.route.own
        if own is None:
            far(0)
        elif isinstance(own, str):
            near()
        else:

            @pl.when(own)
            def _():
                near()

            @pl.when(jnp.logical_not(own))
            def _():
                far(0)

        if self.route.count > 1:
            loop(1, self.route.count, far)

    def start(self):
        self.each(lambda i: self.copy(i).start(), lambda: self.local().start())

    def wait_slot(self, k):
        pltpu.make_async_copy(self.dst(k), self.dst(k), self.recv_sem.at[k]).wait()

    def wait_recv(self):
        if self.route.count == 1:
            self.wait_slot(0)
        else:
            loop(0, self.route.count, self.wait_slot)

    def wait_send(self):
        self.each(lambda i: self.copy(i).wait_send(), lambda: None)


def sems(n):
    return [pltpu.SemaphoreType.DMA((n,)), pltpu.SemaphoreType.DMA((n,))]


def call(kernel, outs, counts, ident, args):
    return pl.pallas_call(
        kernel,
        out_shape=[jax.ShapeDtypeStruct(s, d) for s, d in outs],
        in_specs=[pl.BlockSpec(memory_space=pl.ANY)] * len(args),
        out_specs=[pl.BlockSpec(memory_space=pl.ANY)] * len(outs),
        scratch_shapes=sum([sems(n) for n in counts], []),
        compiler_params=pltpu.CompilerParams(collective_id=ident, has_side_effects=True),
        name="exchange_%d" % ident,
    )(*args)


def run(transfers):
    for t in transfers:
        t.start()
    for t in transfers:
        t.wait_recv()
    for t in transfers:
        t.wait_send()


def spread_kernel(q, p, ids, qh, ph, idh, pp, qq, s0, r0, s1, r1, s2, r2, s3, r3, s4, r4, s5, r5):
    table = routes()
    y, dp, z, x, c = place()
    enter(["holder", "plane_core", "to_query", "to_passage", "sibling"], table)
    hold = Transfer(table["holder"], lambda i: q, lambda k: qh.at[c, k], s0, r0)
    hold_ids = Transfer(table["holder"], lambda i: ids, lambda k: idh.at[k], s1, r1)
    pass_on = Transfer(table["plane_core"], lambda i: p, lambda k: ph.at[k], s2, r2)
    pair_p = Transfer(table["to_query"], lambda i: p, lambda k: pp, s3, r3)
    pair_q = Transfer(table["to_passage"], lambda i: q, lambda k: qq, s4, r4)
    for t in (hold_ids, hold, pass_on, pair_p, pair_q):
        t.start()

    def forward(k):
        return pltpu.make_async_remote_copy(
            src_ref=qh.at[c, k],
            dst_ref=qh.at[c, k],
            send_sem=s5.at[k],
            recv_sem=r5.at[k],
            device_id=(y, dp + 1 - 2 * c),
            device_id_type=MESH,
        )

    def hand(k):
        hold.wait_slot(k)
        forward(k).start()

    loop(0, 8, hand)

    def taken(k):
        pltpu.make_async_copy(qh.at[1 - c, k], qh.at[1 - c, k], r5.at[k]).wait()

    loop(0, 8, taken)
    for t in (hold_ids, pass_on, pair_p, pair_q):
        t.wait_recv()
    for t in (hold_ids, hold, pass_on, pair_p, pair_q):
        t.wait_send()
    loop(0, 8, lambda k: forward(k).wait_send())


def ask_kernel(xs, rows, sums, pos, xo, rowo, sumo, poso, s0, r0, s1, r1, s2, r2, s3, r3):
    table = routes()
    enter(["plane", "zcore", "holder"], table)
    plane = table["plane"]
    run(
        [
            Transfer(table["zcore"], lambda i: sums, lambda k: sumo.at[k], s2, r2),
            Transfer(table["holder"], lambda i: pos, lambda k: poso.at[k], s3, r3),
            Transfer(plane, lambda i: rows.at[plane.item(i)], lambda k: rowo.at[k], s1, r1),
            Transfer(plane, lambda i: xs.at[plane.item(i)], lambda k: xo.at[k], s0, r0),
        ]
    )


def answer_kernel(ys, es, part, yo, eo, parto, s0, r0, s1, r1, s2, r2):
    table = routes()
    enter(["plane", "sibling"], table)
    plane = table["plane"]
    run(
        [
            Transfer(plane, lambda i: es.at[plane.item(i)], lambda k: eo.at[k], s1, r1),
            Transfer(table["sibling"], lambda i: part, lambda k: parto, s2, r2),
            Transfer(plane, lambda i: ys.at[plane.item(i)], lambda k: yo.at[k], s0, r0),
        ]
    )


def total_kernel(tot, line, homes, s0, r0, s1, r1):
    table = routes()
    enter(["zline", "home"], table)
    run(
        [
            Transfer(table["zline"], lambda i: tot, lambda k: line.at[k], s0, r0),
            Transfer(table["home"], lambda i: tot, lambda k: homes.at[k], s1, r1),
        ]
    )


def finish_kernel(zs, inv, gs, pw, zo, invo, go, pwo, s0, r0, s1, r1, s2, r2, s3, r3):
    table = routes()
    enter(["home", "plane", "plane_core", "to_passage"], table)
    home, plane, core = table["home"], table["plane"], table["plane_core"]
    run(
        [
            Transfer(plane, lambda i: inv.at[plane.item(i)], lambda k: invo.at[k], s1, r1),
            Transfer(table["to_passage"], lambda i: pw, lambda k: pwo, s3, r3),
            Transfer(home, lambda i: zs.at[home.item(i)], lambda k: zo.at[k], s0, r0),
            Transfer(core, lambda i: gs.at[core.item(i)], lambda k: go.at[k], s2, r2),
        ]
    )


def unit_rows(hidden, weight):
    projected = jnp.dot(hidden, weight, preferred_element_type=F32)
    length = jnp.sqrt(jnp.sum(projected * projected, axis=1, keepdims=True) + 1e-06)
    return (projected / length).astype(BF16)


def lanes(values):
    lead, n = values.shape[:-1], values.shape[-1]
    rows = -(-n // 128)
    values = jnp.pad(values, [(0, 0)] * len(lead) + [(0, rows * 128 - n)])
    values = values.reshape(lead + (rows, 128))
    return jnp.pad(values, [(0, 0)] * len(lead) + [(0, 8 - rows), (0, 0)])


def shards(query_hidden, passage_hidden, pool_hidden, query_proj, passage_proj, negative_ids):
    y, dp, z, x, c = place()
    emb = query_proj.shape[1]
    cap = 12
    own_hidden = lax.dynamic_slice_in_dim(query_hidden, y * 48, 48, 0)
    own_ids = lax.dynamic_slice_in_dim(negative_ids, y * 48, 48, 0)
    q48 = unit_rows(own_hidden, query_proj)
    p48 = unit_rows(passage_hidden, passage_proj)
    pool = unit_rows(pool_hidden, passage_proj)
    ids48 = jnp.pad(own_ids.T, ((0, 0), (0, 80)))

    qh, ph, idh, pp, qq = call(
        spread_kernel,
        [((2, 8, 48, emb), BF16), ((16, 48, emb), BF16), ((8, 8, 128), jnp.int32), ((48, emb), BF16), ((48, emb), BF16)],
        [8, 8, 16, 1, 1, 8],
        1,
        [q48, p48, ids48],
    )
    q_all = qh.reshape(768, emb)
    q_own = lax.dynamic_index_in_dim(qh, c, 0, keepdims=False).reshape(384, emb)
    p_all = ph.reshape(768, emb)

    ids = idh[:, :, :48].reshape(2, 4, 8, 48).transpose(0, 2, 1, 3).reshape(2, 8, 192)
    owner, local_row = ids // 512, ids % 512
    in_plane = (owner // 8) % 8 == z
    target = jnp.where(in_plane, (owner // 64) * 8 + owner % 8, -1)
    names = (target[:, :, None, :] == jnp.arange(PLANE, dtype=jnp.int32)[None, None, :, None]).astype(F32)
    per_query = jnp.sum(names, axis=1)
    before = (jnp.arange(192)[:, None] < jnp.arange(192)[None, :]).astype(BF16)
    earlier = lax.dot_general(
        per_query.astype(BF16).reshape(2 * PLANE, 192), before, (((1,), (0,)), ((), ())), preferred_element_type=F32
    ).reshape(2, PLANE, 192)
    ranks = []
    running = earlier
    for k in range(8):
        ranks.append(jnp.sum(names[:, k] * running, axis=1))
        running = running + names[:, k]
    rank = jnp.stack(ranks, axis=1).astype(jnp.int32)
    half = jnp.arange(2, dtype=jnp.int32)[:, None, None]
    slot = jnp.where(in_plane, target * (2 * cap) + half * cap + rank, -1)
    slot = slot.transpose(1, 0, 2).reshape(8, 384)
    row_code = (local_row + 1).transpose(1, 0, 2).reshape(8, 384)
    slot_ids = jnp.arange(PLANE * 2 * cap, dtype=jnp.int32)[:, None]
    pick = jnp.zeros((768, 384), F32)
    for k in range(8):
        hit = slot[k][None, :] == slot_ids
        pick = jnp.where(hit, 1.0, pick)
    pick = pick.astype(BF16)
    row_of = jnp.sum(
        sum(jnp.where(slot[k][None, :] == slot_ids, row_code[k][None, :], 0) for k in range(8)), axis=1
    )
    asked = jnp.dot(pick, q_own, preferred_element_type=F32).astype(BF16)

    scores = logit_scale * lax.dot_general(q_all, p_all, (((1,), (1,)), ((), ())), preferred_element_type=F32)
    exp_scores = jnp.exp(scores)
    row_sums = jnp.sum(exp_scores, axis=1)
    exp_low = exp_scores.astype(BF16)
    pos_exp = jnp.exp(logit_scale * jnp.sum(q48.astype(F32) * pp.astype(F32), axis=1))

    xo, rowo, sumo, poso = call(
        ask_kernel,
        [((32, 24, emb), BF16), ((32, 8, 128), jnp.int32), ((16, 8, 128), F32), ((8, 8, 128), F32)],
        [32, 32, 16, 8],
        2,
        [asked.reshape(32, 24, emb), lanes(row_of.reshape(32, 24)), lanes(row_sums), lanes(pos_exp)],
    )
    x_rows = xo.reshape(768, emb)
    row_code_o = rowo[:, 0, :24].reshape(768)
    chosen = (row_code_o[None, :] == jnp.arange(1, 513, dtype=jnp.int32)[:, None]).astype(BF16)
    named = lax.dot_general(chosen, pool, (((0,), (0,)), ((), ())), preferred_element_type=F32)
    neg_exp = jnp.exp(logit_scale * jnp.sum(x_rows.astype(F32) * named, axis=1))
    weighted = (neg_exp[:, None] * named).astype(BF16)

    inv_batch = 1.0 / jnp.sum(sumo, axis=0)[:6].reshape(768)
    query_part = jnp.dot(exp_low, p_all, preferred_element_type=F32).reshape(2, 384, emb)
    mine = lax.dynamic_index_in_dim(query_part, c, 0, keepdims=False)
    theirs = lax.dynamic_index_in_dim(query_part, 1 - c, 0, keepdims=False).astype(BF16)
    scaled_q = (q_all.astype(F32) * inv_batch[:, None]).astype(BF16)
    passage_part = lax.dot_general(exp_low, scaled_q, (((0,), (0,)), ((), ())), preferred_element_type=F32)

    yo, eo, sib = call(
        answer_kernel,
        [((32, 24, emb), BF16), ((32, 8, 128), F32), ((384, emb), BF16)],
        [32, 32, 1],
        3,
        [weighted.reshape(32, 24, emb), lanes(neg_exp.reshape(32, 24)), theirs],
    )
    hard_rows = lax.dot_general(pick, yo.reshape(768, emb), (((0,), (0,)), ((), ())), preferred_element_type=F32)
    neg_total = jnp.dot(
        eo[:, 0, :24].reshape(1, 768), pick.astype(F32), precision=lax.Precision.HIGHEST, preferred_element_type=F32
    ).reshape(384)

    line, homes = call(
        total_kernel, [((8, 8, 128), F32), ((8, 8, 128), F32)], [8, 8], 4, [lanes(neg_total)]
    )
    pos_held = poso[:, 0, :48].reshape(384)
    inv_hard = 1.0 / (jnp.sum(line, axis=0)[:3].reshape(384) + pos_held)
    inv_own = lax.dynamic_index_in_dim(inv_batch.reshape(2, 384), c, 0, keepdims=False)
    query_sum = (
        (mine + sib.astype(F32)) * inv_own[:, None] + hard_rows * inv_hard[:, None]
    ).astype(BF16)
    inv_slots = jnp.dot(
        inv_hard.reshape(1, 384), pick.astype(F32).T, precision=lax.Precision.HIGHEST, preferred_element_type=F32
    ).reshape(32, 24)
    home_total = jnp.sum(homes, axis=0)[:3].reshape(8, 48)
    home_total = lax.dynamic_index_in_dim(home_total, (z % 2) * 4 + y, 0, keepdims=False)
    pos_coef = pos_exp / (pos_exp + home_total) - 2.0

    zo, invo, go, pwo = call(
        finish_kernel,
        [((8, 48, emb), BF16), ((32, 8, 128), F32), ((16, 48, emb), BF16), ((8, 128), F32)],
        [8, 32, 16, 1],
        5,
        [query_sum.reshape(8, 48, emb), lanes(inv_slots), passage_part.astype(BF16).reshape(16, 48, emb), lanes(pos_coef)],
    )
    query_grad = logit_scale * (jnp.sum(zo.astype(F32), axis=0) + pos_coef[:, None] * pp.astype(F32))
    passage_grad = logit_scale * (jnp.sum(go.astype(F32), axis=0) + pwo[0, :48][:, None] * qq.astype(F32))
    hard_weight = neg_exp * invo[:, 0, :24].reshape(768)
    spread = (chosen.astype(F32) * hard_weight[None, :]).astype(BF16)
    negative_grad = logit_scale * jnp.dot(spread, x_rows, preferred_element_type=F32)
    return query_grad.astype(BF16), passage_grad.astype(BF16), negative_grad.astype(BF16)


def solution(mesh):
    placed = (
        P("dp", None),
        P(("tower", "dp"), None),
        P(("tower", "dp"), None),
        P(),
        P(),
        P("dp", None),
    )
    return jax.shard_map(
        shards,
        mesh=mesh,
        in_specs=placed,
        out_specs=(P(("dp", "tower"), None), P(("tower", "dp"), None), P(("tower", "dp"), None)),
        check_vma=False,
    )
```

```python
import jax
import jax.numpy as jnp
from jax import lax
from jax.experimental import pallas as pl
from jax.experimental.pallas import tpu as pltpu
from jax.sharding import PartitionSpec as P

logit_scale = 50.0
MESH = pl.DeviceIdType.MESH
F32 = jnp.float32
BF16 = jnp.bfloat16
I32 = jnp.int32
EMB = 768
CAP = 12
SLOTS = 2 * CAP
QB = 48
QD = 192
NN = (((1,), (0,)), ((), ()))
NT = (((1,), (1,)), ((), ()))
TN = (((0,), (0,)), ((), ()))


def mm(a, b, dims=NN):
    return lax.dot_general(a, b, dims, preferred_element_type=F32)


def rem(a, n):
    return lax.rem(a, n)


def quo(a, n):
    return lax.div(a, n)


def loop(lo, hi, body):
    def step(i, carry):
        body(i)
        return carry

    lax.fori_loop(lo, hi, step, 0)


def place():
    y = lax.axis_index("tower")
    dp = lax.axis_index("dp")
    return y, dp, quo(dp, 8), rem(quo(dp, 2), 4), rem(dp, 2)


class Route:
    def __init__(self, count, dest, source, slot, own, item=None):
        self.count, self.dest, self.source = count, dest, source
        self.slot, self.own, self.item = slot, own, item


def make_routes():
    y, dp, z, x, c = place()
    line = x * 2 + c
    turn = rem(y + 8 - z, 4)
    lead = quo(z, 4) * 4 + y
    at_home = rem(2 * z, 4) == y

    def plane_core(i):
        n = rem(y * 4 + x + i, 16)
        return quo(n, 4), z * 8 + rem(n, 4) * 2 + c

    def zcore(i):
        g = rem(z * 2 + c + i, 16)
        zz = quo(g, 2)
        return rem(turn + zz, 4), zz * 8 + x * 2 + rem(g, 2)

    def zline(i):
        zz = rem(z + i, 8)
        return rem(turn + zz, 4), zz * 8 + line

    def holder(i):
        zz = rem(z + i, 8)
        return rem(z + zz, 4), zz * 8 + line

    def home(i):
        k = rem(lead + i, 8)
        return rem(k, 4), (turn + 4 * quo(k, 4)) * 8 + line

    to_query = (rem(dp, 4), y * 16 + quo(dp, 4))
    to_passage = (quo(dp, 16), rem(dp, 16) * 4 + y)
    query_own = (to_query[0] == y) & (to_query[1] == dp)
    passage_own = (to_passage[0] == y) & (to_passage[1] == dp)
    return {
        "plane_core": Route(16, plane_core, plane_core, y * 4 + x, True, lambda i: rem(y * 4 + x + i, 16)),
        "zline": Route(8, zline, zline, z, True),
        "zcore": Route(16, zcore, zcore, z * 2 + c, True),
        "holder": Route(8, holder, home, lead, at_home),
        "home": Route(8, home, holder, z, at_home, lambda i: rem(lead + i, 8)),
        "to_query": Route(1, lambda i: to_query, lambda i: to_passage, 0, query_own),
        "to_passage": Route(1, lambda i: to_passage, lambda i: to_query, 0, passage_own),
    }


def each(route, far, near):
    if route.own is True:
        near()
    else:

        @pl.when(route.own)
        def _():
            near()

        @pl.when(jnp.logical_not(route.own))
        def _():
            far(0)

    if route.count > 1:
        loop(1, route.count, far)


class Transfer:
    def __init__(self, route, src, dst, sems):
        self.route, self.src, self.dst = route, src, dst
        self.send_sem, self.recv_sem = sems

    def copy(self, i):
        slot = self.route.slot
        return pltpu.make_async_remote_copy(
            src_ref=self.src(i),
            dst_ref=self.dst(slot),
            send_sem=self.send_sem.at[i],
            recv_sem=self.recv_sem.at[slot],
            device_id=self.route.dest(i),
            device_id_type=MESH,
        )

    def local(self):
        slot = self.route.slot
        return pltpu.make_async_copy(self.src(0), self.dst(slot), self.recv_sem.at[slot])

    def start(self):
        each(self.route, lambda i: self.copy(i).start(), lambda: self.local().start())

    def wait_slot(self, k):
        pltpu.make_async_copy(self.dst(k), self.dst(k), self.recv_sem.at[k]).wait()

    def wait_recv(self):
        loop(0, self.route.count, self.wait_slot)

    def wait_send(self):
        each(self.route, lambda i: self.copy(i).wait_send(), lambda: None)


class PlaneTransfer:
    def __init__(self, src, dst, sems):
        self.src, self.dst = src, dst
        self.send_sem, self.recv_sem = sems
        y, dp, z, x, c = place()
        self.base, self.line, self.me = z * 8, x * 2 + c, y * 8 + x * 2 + c

    def copy(self, row, spot):
        m = row * 8 + spot
        return pltpu.make_async_remote_copy(
            src_ref=self.src.at[m],
            dst_ref=self.dst.at[self.me],
            send_sem=self.send_sem.at[m],
            recv_sem=self.recv_sem.at[self.me],
            device_id=(row, self.base + spot),
            device_id_type=MESH,
        )

    def start_row(self, row):
        def go(t):
            spot = rem(self.line + t, 8)
            own = row * 8 + spot == self.me

            @pl.when(own)
            def _():
                pltpu.make_async_copy(
                    self.src.at[self.me], self.dst.at[self.me], self.recv_sem.at[self.me]
                ).start()

            @pl.when(jnp.logical_not(own))
            def _():
                self.copy(row, spot).start()

        loop(0, 8, go)

    def wait_row(self, row):
        def take(t):
            m = row * 8 + t
            pltpu.make_async_copy(self.dst.at[m], self.dst.at[m], self.recv_sem.at[m]).wait()

        loop(0, 8, take)

    def wait_send(self):
        def done(m):
            @pl.when(m != self.me)
            def _():
                self.copy(quo(m, 8), rem(m, 8)).wait_send()

        loop(0, 32, done)


def lane_of(shape):
    return lax.broadcasted_iota(I32, shape, len(shape) - 1)


def pack(column, base=0):
    groups = column.shape[0] // 8
    lane = lane_of((8, 128)) - base
    tile = jnp.zeros((8, 128), F32)
    for g in range(groups):
        tile = jnp.where(lane == g, column[8 * g : 8 * g + 8], tile)
    return tile


def unpack(tile, groups, base=0):
    lane = lane_of((8, 128)) - base
    parts = [jnp.sum(jnp.where(lane == g, tile, 0.0), axis=1, keepdims=True) for g in range(groups)]
    return jnp.concatenate(parts, axis=0)


def pack_slots(column):
    split = column.reshape(8, 3, 8, 1)
    lane = lane_of((8, 8, 128))
    tile = jnp.zeros((8, 8, 128), F32)
    for g in range(3):
        tile = jnp.where(lane == g, split[:, g], tile)
    return tile


def unpack_slots(tile):
    lane = lane_of((8, 8, 128))
    parts = [jnp.sum(jnp.where(lane == g, tile, 0.0), axis=2, keepdims=True)[:, None] for g in range(3)]
    return jnp.concatenate(parts, axis=1).reshape(QD, 1)


def three_parts(column):
    high = column.astype(BF16).astype(F32)
    rest = column - high
    middle = rest.astype(BF16).astype(F32)
    low = rest - middle
    lane = lane_of((column.shape[0], 128))
    parts = jnp.where(lane == 0, high, jnp.where(lane == 1, middle, jnp.where(lane == 2, low, 0.0)))
    return parts.astype(BF16)


def unit(projected):
    length = jnp.sqrt(jnp.sum(projected * projected, axis=1, keepdims=True) + 1e-06)
    return (projected / length).astype(BF16)


def flat(block):
    return block.astype(F32).reshape(block.shape[0] * block.shape[1], EMB)


SCRATCH = dict(
    wq=((2304, EMB), BF16),
    wp=((3072, EMB), BF16),
    hq=((QB, 2304), BF16),
    hp=((QB, 3072), BF16),
    hpool=((512, 3072), BF16),
    q48=((QB, EMB), BF16),
    p48=((QB, EMB), BF16),
    pool=((512, EMB), BF16),
    ids=((8, 256), I32),
    idh=((8, 8, 256), I32),
    qh=((2, 8, QB, EMB), BF16),
    ph=((16, QB, EMB), BF16),
    pp=((QB, EMB), BF16),
    qq=((QB, EMB), BF16),
    pick=((2, 768, QD), BF16),
    xs=((32, SLOTS, EMB), BF16),
    xr=((32, SLOTS, EMB), BF16),
    rs=((32, 8, 128), F32),
    rr=((32, 8, 128), F32),
    e=((768, 768), BF16),
    sums=((8, 128), F32),
    sumr=((16, 8, 128), F32),
    pos=((8, 128), F32),
    posr=((8, 8, 128), F32),
    nq=((768, EMB), F32),
    ns=((384, EMB), BF16),
    nr=((384, EMB), BF16),
    qn=((768, EMB), BF16),
    gs=((768, EMB), BF16),
    gr=((16, QB, EMB), BF16),
    chosen=((768, 512), BF16),
    ys=((32, SLOTS, EMB), BF16),
    yr=((32, SLOTS, EMB), BF16),
    es=((32, 8, 128), F32),
    er=((32, 8, 128), F32),
    tot=((8, 128), F32),
    totl=((8, 8, 128), F32),
    toth=((8, 8, 128), F32),
    invs=((32, 8, 128), F32),
    invr=((32, 8, 128), F32),
    hard=((2, QD, EMB), F32),
    zs=((8, QB, EMB), BF16),
    zr=((8, QB, EMB), BF16),
    pws=((8, 128), F32),
    pwr=((8, 128), F32),
    xw=((768, EMB), BF16),
)
PAIRS = dict(
    ids=8, q=8, p=16, pp=1, qq=1, fwd=8, x=32, r=32, sums=16, pos=8, n=1, y=32, e=32, totl=8, toth=8, inv=32, z=8,
    g=16, pw=1,
)


class Bag:
    pass


def step_kernel(wq, wp, hq, hp, hpool, ids, oq, op, on, *refs):
    v = Bag()
    for name, ref in zip(SCRATCH, refs):
        setattr(v, name, ref)
    rest = refs[len(SCRATCH) :]
    s = {name: (rest[2 * i], rest[2 * i + 1]) for i, name in enumerate(PAIRS)}
    in_sem = rest[2 * len(PAIRS)]
    routes = make_routes()
    y, dp, z, x, c = place()
    line = x * 2 + c
    turn = rem(y + 8 - z, 4)
    lead = quo(z, 4) * 4 + y

    inputs = [
        (ids, v.ids),
        (hq.at[pl.ds(pl.multiple_of(y * QB, QB), QB)], v.hq),
        (wq, v.wq),
        (hp, v.hp),
        (wp, v.wp),
        (hpool, v.hpool),
    ]
    loads = [pltpu.make_async_copy(a, b, in_sem.at[i]) for i, (a, b) in enumerate(inputs)]
    for load in loads:
        load.start()

    barrier = pltpu.get_barrier_semaphore()

    def greet(ty, td):
        pl.semaphore_signal(barrier, inc=1, device_id=(ty, td), device_id_type=MESH)

    wanted = 0
    for name in ("holder", "home", "to_query", "to_passage", "zcore"):
        route = routes[name]
        each(route, lambda i, route=route: greet(*route.source(i)), lambda: None)
        wanted = wanted + route.count - 1
        if route.own is not True:
            wanted = wanted + jnp.where(route.own, 0, 1)

    def greet_plane(i):
        m = rem(y * 8 + line + i, 32)
        greet(quo(m, 8), z * 8 + rem(m, 8))

    loop(1, 32, greet_plane)
    wanted = wanted + 31

    for i in (0, 1, 2):
        loads[i].wait()
    v.q48[...] = unit(mm(v.hq[...], v.wq[...]))
    pl.semaphore_wait(barrier, wanted)
    t_ids = Transfer(routes["holder"], lambda i: v.ids, lambda k: v.idh.at[k], s["ids"])
    t_q = Transfer(routes["holder"], lambda i: v.q48, lambda k: v.qh.at[c, k], s["q"])
    t_qq = Transfer(routes["to_passage"], lambda i: v.q48, lambda k: v.qq, s["qq"])
    t_ids.start()
    t_q.start()
    t_qq.start()
    for i in (3, 4):
        loads[i].wait()
    v.p48[...] = unit(mm(v.hp[...], v.wp[...]))
    t_p = Transfer(routes["plane_core"], lambda i: v.p48, lambda k: v.ph.at[k], s["p"])
    t_pp = Transfer(routes["to_query"], lambda i: v.p48, lambda k: v.pp, s["pp"])
    t_pp.start()
    t_p.start()
    loads[5].wait()

    def project_pool(i):
        part = pl.ds(pl.multiple_of(i * 256, 256), 256)
        v.pool[part, :] = unit(mm(v.hpool[part, :], v.wp[...]))

    loop(0, 2, project_pool)

    t_ids.wait_recv()
    before = (lax.broadcasted_iota(I32, (QD, QD), 0) < lane_of((QD, QD))).astype(F32).astype(BF16)
    member_row = lax.broadcasted_iota(I32, (32, QD), 0)
    slots, codes = [], []
    for half in range(2):
        held = v.idh[4 * half][:, :QD]
        owner = lax.shift_right_logical(held, 9)
        inside = (lax.shift_right_logical(owner, 3) & 7) == z
        target = jnp.where(inside, lax.shift_right_logical(owner, 6) * 8 + (owner & 7), -1)
        code = ((held & 511) + 1).astype(F32)
        names = [(member_row == target[k : k + 1]).astype(F32) for k in range(8)]
        count = names[0]
        for k in range(1, 8):
            count = count + names[k]
        running = mm(count.astype(BF16), before)
        start = (target * SLOTS + half * CAP).astype(F32)
        rows = []
        for k in range(8):
            rank = jnp.sum(names[k] * running, axis=0, keepdims=True)
            rows.append(jnp.where(target[k : k + 1] >= 0, start[k : k + 1] + rank, -1.0))
            running = running + names[k]
        slots.append(rows)
        codes.append([code[k : k + 1] for k in range(8)])

    def forward(k):
        return pltpu.make_async_remote_copy(
            src_ref=v.qh.at[c, k],
            dst_ref=v.qh.at[c, k],
            send_sem=s["fwd"][0].at[k],
            recv_sem=s["fwd"][1].at[k],
            device_id=(y, dp + 1 - 2 * c),
            device_id_type=MESH,
        )

    def hand_on(k):
        t_q.wait_slot(k)
        forward(k).start()

    loop(0, 8, hand_on)

    t_x = PlaneTransfer(v.xs, v.xr, s["x"])
    t_r = PlaneTransfer(v.rs, v.rr, s["r"])

    def ask(j):
        row = rem(y + j, 4)
        here = pl.ds(pl.multiple_of(row * QD, QD), QD)
        spot = (lax.broadcasted_iota(I32, (QD, QD), 0) + row * QD).astype(F32)
        found = jnp.zeros((QD, QD), F32)
        asked = jnp.zeros((QD, EMB), F32)
        for half in range(2):
            hits = jnp.zeros((QD, QD), F32)
            for k in range(8):
                hits = jnp.where(spot == slots[half][k], codes[half][k], hits)
            found = found + hits
            picked = jnp.where(hits > 0.0, 1.0, 0.0).astype(BF16)
            v.pick[half, here, :] = picked
            asked = asked + mm(picked, v.qh[c, 4 * half : 4 * half + 4].reshape(QD, EMB))
        v.xs[pl.ds(row * 8, 8)] = asked.reshape(8, SLOTS, EMB).astype(BF16)
        v.rs[pl.ds(row * 8, 8)] = pack_slots(jnp.sum(found, axis=1, keepdims=True))
        t_r.start_row(row)
        t_x.start_row(row)

    loop(0, 4, ask)

    t_pp.wait_recv()
    pos_exp = jnp.exp(logit_scale * jnp.sum(v.q48[...].astype(F32) * v.pp[...].astype(F32), axis=1, keepdims=True))
    v.pos[...] = pack(pos_exp, lead * 6)
    t_pos = Transfer(routes["holder"], lambda i: v.pos, lambda k: v.posr.at[k], s["pos"])
    t_pos.start()

    t_p.wait_recv()

    def taken(k):
        pltpu.make_async_copy(v.qh.at[1 - c, k], v.qh.at[1 - c, k], s["fwd"][1].at[k]).wait()

    loop(0, 8, taken)

    def queries(j):
        return v.qh[quo(j, 2), pl.ds(rem(j, 2) * 4, 4)].reshape(QD, EMB)

    def score(j, tile):
        here = pl.ds(pl.multiple_of(j * QD, QD), QD)
        passages = v.ph[...].reshape(768, EMB)
        grown = jnp.exp(logit_scale * mm(queries(j), passages, NT))
        low = grown.astype(BF16)
        v.e[here, :] = low
        v.nq[here, :] = mm(low, passages)
        return tile + pack(jnp.sum(grown, axis=1, keepdims=True), j * 24)

    v.sums[...] = lax.fori_loop(0, 4, score, jnp.zeros((8, 128), F32))
    t_sums = Transfer(routes["zcore"], lambda i: v.sums, lambda k: v.sumr.at[k], s["sums"])
    t_sums.start()
    v.ns[...] = v.nq[pl.ds(pl.multiple_of((1 - c) * 384, 384), 384), :].astype(BF16)
    send_n = pltpu.make_async_remote_copy(
        src_ref=v.ns,
        dst_ref=v.nr,
        send_sem=s["n"][0].at[0],
        recv_sem=s["n"][1].at[0],
        device_id=(y, dp + 1 - 2 * c),
        device_id_type=MESH,
    )
    send_n.start()
    t_sums.wait_recv()
    inv_batch = 1.0 / jnp.where(lane_of((8, 128)) < 96, jnp.sum(v.sumr[...], axis=0), 1.0)

    def scale_queries(j):
        here = pl.ds(pl.multiple_of(j * QD, QD), QD)
        v.qn[here, :] = (queries(j).astype(F32) * unpack(inv_batch, 24, j * 24)).astype(BF16)

    loop(0, 4, scale_queries)
    for j in range(3):
        v.gs[256 * j : 256 * j + 256, :] = mm(v.e[:, 256 * j : 256 * j + 256], v.qn[...], TN).astype(BF16)

    t_y = PlaneTransfer(v.ys, v.yr, s["y"])
    t_e = PlaneTransfer(v.es, v.er, s["e"])

    def answer(j):
        row = rem(y + 4 - j, 4)
        here = pl.ds(pl.multiple_of(row * QD, QD), QD)
        t_r.wait_row(row)
        t_x.wait_row(row)
        code = unpack_slots(v.rr[pl.ds(row * 8, 8)])
        chosen = jnp.where(code == (lane_of((QD, 512)) + 1).astype(F32), 1.0, 0.0).astype(BF16)
        v.chosen[here, :] = chosen
        named = mm(chosen, v.pool[...])
        asked = flat(v.xr[pl.ds(row * 8, 8)])
        neg_exp = jnp.exp(logit_scale * jnp.sum(asked * named, axis=1, keepdims=True))
        v.es[pl.ds(row * 8, 8)] = pack_slots(neg_exp)
        t_e.start_row(row)
        v.ys[pl.ds(row * 8, 8)] = (neg_exp * named).reshape(8, SLOTS, EMB).astype(BF16)
        t_y.start_row(row)

    loop(0, 4, answer)

    def total(j, carry):
        row = rem(y + j, 4)
        here = pl.ds(pl.multiple_of(row * QD, QD), QD)
        t_e.wait_row(row)
        parts = three_parts(unpack_slots(v.er[pl.ds(row * 8, 8)]))
        return tuple(carry[half] + mm(v.pick[half, here, :], parts, TN) for half in range(2))

    both = lax.fori_loop(0, 4, total, (jnp.zeros((QD, 128), F32), jnp.zeros((QD, 128), F32)))
    column = jnp.concatenate([jnp.sum(t, axis=1, keepdims=True) for t in both], axis=0)
    v.tot[...] = pack(column)
    t_totl = Transfer(routes["zline"], lambda i: v.tot, lambda k: v.totl.at[k], s["totl"])
    t_toth = Transfer(routes["home"], lambda i: v.tot, lambda k: v.toth.at[k], s["toth"])
    t_totl.start()
    t_toth.start()
    t_pos.wait_recv()
    t_totl.wait_recv()
    hard_total = jnp.sum(v.totl[...], axis=0) + jnp.sum(v.posr[...], axis=0)
    inv_hard_tile = 1.0 / jnp.where(lane_of((8, 128)) < 48, hard_total, 1.0)
    inv_hard = [unpack(inv_hard_tile, 24, 24 * half) for half in range(2)]
    inv_parts = [three_parts(inv_hard[half]) for half in range(2)]
    t_inv = PlaneTransfer(v.invs, v.invr, s["inv"])

    def tell(j):
        row = rem(y + j, 4)
        here = pl.ds(pl.multiple_of(row * QD, QD), QD)
        shares = mm(v.pick[0, here, :], inv_parts[0]) + mm(v.pick[1, here, :], inv_parts[1])
        v.invs[pl.ds(row * 8, 8)] = pack_slots(jnp.sum(shares, axis=1, keepdims=True))
        t_inv.start_row(row)

    loop(0, 4, tell)
    t_toth.wait_recv()
    own_total = unpack(jnp.sum(v.toth[...], axis=0), 6, lead * 6)
    pos_coef = pos_exp / (pos_exp + own_total) - 2.0
    v.pws[...] = pack(pos_coef)
    t_pw = Transfer(routes["to_passage"], lambda i: v.pws, lambda k: v.pwr, s["pw"])
    t_pw.start()

    v.hard[...] = jnp.zeros((2, QD, EMB), F32)

    def collect(j):
        row = rem(y + j, 4)
        here = pl.ds(pl.multiple_of(row * QD, QD), QD)
        t_y.wait_row(row)
        rows = flat(v.yr[pl.ds(row * 8, 8)]).astype(BF16)
        for half in range(2):
            v.hard[half] += mm(v.pick[half, here, :], rows, TN)

    loop(0, 4, collect)
    pltpu.make_async_copy(v.nr, v.nr, s["n"][1].at[0]).wait()
    t_z = Transfer(routes["home"], lambda i: v.zs.at[routes["home"].item(i)], lambda k: v.zr.at[k], s["z"])
    for half in range(2):
        mine = v.nq[pl.ds(pl.multiple_of(c * 384 + half * QD, QD), QD), :] + v.nr[half * QD : half * QD + QD, :].astype(F32)
        inv_own = unpack(inv_batch, 24, c * 48 + half * 24)
        mixed = mine * inv_own + v.hard[half] * inv_hard[half]
        v.zs[4 * half : 4 * half + 4] = mixed.astype(BF16).reshape(4, QB, EMB)
    t_z.start()
    core = routes["plane_core"]
    t_g = Transfer(
        core,
        lambda i: v.gs.at[pl.ds(pl.multiple_of(core.item(i) * QB, QB), QB), :],
        lambda k: v.gr.at[k],
        s["g"],
    )
    t_g.start()

    def weigh(j):
        row = rem(y + 4 - j, 4)
        here = pl.ds(pl.multiple_of(row * QD, QD), QD)
        t_inv.wait_row(row)
        share = unpack_slots(v.es[pl.ds(row * 8, 8)]) * unpack_slots(v.invr[pl.ds(row * 8, 8)])
        v.xw[here, :] = (flat(v.xr[pl.ds(row * 8, 8)]) * share).astype(BF16)

    loop(0, 4, weigh)
    for j in range(2):
        part = mm(v.chosen[:, 256 * j : 256 * j + 256], v.xw[...], TN)
        on[256 * j : 256 * j + 256, :] = (logit_scale * part).astype(BF16)

    t_z.wait_recv()
    summed = jnp.sum(v.zr[...].astype(F32), axis=0)
    oq[...] = (logit_scale * (summed + pos_coef * v.pp[...].astype(F32))).astype(BF16)
    t_pw.wait_recv()
    t_qq.wait_recv()
    t_g.wait_recv()
    summed = jnp.sum(v.gr[...].astype(F32), axis=0)
    coef = unpack(v.pwr[...], 6)
    op[...] = (logit_scale * (summed + coef * v.qq[...].astype(F32))).astype(BF16)

    for t in (t_ids, t_q, t_qq, t_pp, t_p, t_r, t_x, t_pos, t_sums, t_e, t_y, t_totl, t_toth, t_inv, t_pw, t_z, t_g):
        t.wait_send()
    loop(0, 8, lambda k: forward(k).wait_send())
    send_n.wait_send()


def shards(query_hidden, passage_hidden, pool_hidden, query_proj, passage_proj, negative_ids):
    ids = jnp.pad(negative_ids.T, ((0, 0), (0, 64)))
    scratch = [pltpu.VMEM(shape, dtype) for shape, dtype in SCRATCH.values()]
    for n in PAIRS.values():
        scratch += [pltpu.SemaphoreType.DMA((n,)), pltpu.SemaphoreType.DMA((n,))]
    scratch.append(pltpu.SemaphoreType.DMA((6,)))
    return pl.pallas_call(
        step_kernel,
        out_shape=[jax.ShapeDtypeStruct((n, EMB), BF16) for n in (QB, QB, 512)],
        in_specs=[pl.BlockSpec(memory_space=pl.ANY)] * 6,
        out_specs=[pl.BlockSpec(memory_space=pltpu.VMEM)] * 3,
        scratch_shapes=scratch,
        compiler_params=pltpu.CompilerParams(
            collective_id=1, has_side_effects=True, vmem_limit_bytes=60 * 1024 * 1024
        ),
        name="contrastive_step",
    )(query_proj, passage_proj, query_hidden, passage_hidden, pool_hidden, ids)


def solution(mesh):
    placed = (
        P("dp", None),
        P(("tower", "dp"), None),
        P(("tower", "dp"), None),
        P(),
        P(),
        P("dp", None),
    )
    return jax.shard_map(
        shards,
        mesh=mesh,
        in_specs=placed,
        out_specs=(P(("dp", "tower"), None), P(("tower", "dp"), None), P(("tower", "dp"), None)),
        check_vma=False,
    )
```

```python
import jax
import jax.numpy as jnp
from jax import lax
from jax.experimental import pallas as pl
from jax.experimental.pallas import tpu as pltpu
from jax.sharding import PartitionSpec as P

logit_scale = 50.0
MESH = pl.DeviceIdType.MESH
F32 = jnp.float32
BF16 = jnp.bfloat16
I32 = jnp.int32
EMB = 768
CAP = 12
SLOTS = 2 * CAP
QB = 48
QD = 192
NN = (((1,), (0,)), ((), ()))
NT = (((1,), (1,)), ((), ()))
TN = (((0,), (0,)), ((), ()))


def mm(a, b, dims=NN):
    return lax.dot_general(a, b, dims, preferred_element_type=F32)


def rem(a, n):
    return lax.rem(a, n)


def quo(a, n):
    return lax.div(a, n)


def loop(lo, hi, body):
    def step(i, carry):
        body(i)
        return carry

    lax.fori_loop(lo, hi, step, 0)


def place():
    y = lax.axis_index("tower")
    dp = lax.axis_index("dp")
    return y, dp, quo(dp, 8), rem(quo(dp, 2), 4), rem(dp, 2)


class Route:
    def __init__(self, count, dest, source, slot, own, item=None):
        self.count, self.dest, self.source = count, dest, source
        self.slot, self.own, self.item = slot, own, item


def make_routes():
    y, dp, z, x, c = place()
    line = x * 2 + c
    turn = rem(y + 8 - z, 4)
    lead = quo(z, 4) * 4 + y
    at_home = rem(2 * z, 4) == y

    def plane_core(i):
        n = rem(y * 4 + x + i, 16)
        return quo(n, 4), z * 8 + rem(n, 4) * 2 + c

    def zcore(i):
        g = rem(z * 2 + c + i, 16)
        zz = quo(g, 2)
        return rem(turn + zz, 4), zz * 8 + x * 2 + rem(g, 2)

    def zline(i):
        zz = rem(z + i, 8)
        return rem(turn + zz, 4), zz * 8 + line

    def holder(i):
        zz = rem(z + i, 8)
        return rem(z + zz, 4), zz * 8 + line

    def column(i):
        return y, (turn + 4 * rem(quo(z, 4) + i, 2)) * 8 + line

    def home(i):
        k = rem(lead + i, 8)
        return rem(k, 4), (turn + 4 * quo(k, 4)) * 8 + line

    to_query = (rem(dp, 4), y * 16 + quo(dp, 4))
    to_passage = (quo(dp, 16), rem(dp, 16) * 4 + y)
    query_own = (to_query[0] == y) & (to_query[1] == dp)
    passage_own = (to_passage[0] == y) & (to_passage[1] == dp)
    return {
        "plane_core": Route(16, plane_core, plane_core, y * 4 + x, True, lambda i: rem(y * 4 + x + i, 16)),
        "zline": Route(8, zline, zline, z, True),
        "zcore": Route(16, zcore, zcore, z * 2 + c, True),
        "column": Route(2, column, column, quo(z, 4), at_home),
        "holder": Route(8, holder, home, lead, at_home),
        "home": Route(8, home, holder, z, at_home, lambda i: rem(lead + i, 8)),
        "to_query": Route(1, lambda i: to_query, lambda i: to_passage, 0, query_own),
        "to_passage": Route(1, lambda i: to_passage, lambda i: to_query, 0, passage_own),
    }


def each(route, far, near):
    if route.own is True:
        near()
    else:

        @pl.when(route.own)
        def _():
            near()

        @pl.when(jnp.logical_not(route.own))
        def _():
            far(0)

    if route.count > 1:
        loop(1, route.count, far)


class Transfer:
    def __init__(self, route, src, dst, sems):
        self.route, self.src, self.dst = route, src, dst
        self.send_sem, self.recv_sem = sems

    def copy(self, i):
        slot = self.route.slot
        return pltpu.make_async_remote_copy(
            src_ref=self.src(i),
            dst_ref=self.dst(slot),
            send_sem=self.send_sem.at[i],
            recv_sem=self.recv_sem.at[slot],
            device_id=self.route.dest(i),
            device_id_type=MESH,
        )

    def local(self):
        slot = self.route.slot
        return pltpu.make_async_copy(self.src(0), self.dst(slot), self.recv_sem.at[slot])

    def start(self):
        each(self.route, lambda i: self.copy(i).start(), lambda: self.local().start())

    def wait_slot(self, k):
        pltpu.make_async_copy(self.dst(k), self.dst(k), self.recv_sem.at[k]).wait()

    def wait_recv(self):
        loop(0, self.route.count, self.wait_slot)

    def wait_send(self):
        each(self.route, lambda i: self.copy(i).wait_send(), lambda: None)


class PlaneTransfer:
    def __init__(self, src, dst, sems):
        self.src, self.dst = src, dst
        self.send_sem, self.recv_sem = sems
        y, dp, z, x, c = place()
        self.base, self.line, self.me = z * 8, x * 2 + c, y * 8 + x * 2 + c

    def copy(self, row, spot):
        m = row * 8 + spot
        return pltpu.make_async_remote_copy(
            src_ref=self.src.at[m],
            dst_ref=self.dst.at[self.me],
            send_sem=self.send_sem.at[m],
            recv_sem=self.recv_sem.at[self.me],
            device_id=(row, self.base + spot),
            device_id_type=MESH,
        )

    def start_row(self, row):
        def go(t):
            spot = rem(self.line + t, 8)
            own = row * 8 + spot == self.me

            @pl.when(own)
            def _():
                pltpu.make_async_copy(
                    self.src.at[self.me], self.dst.at[self.me], self.recv_sem.at[self.me]
                ).start()

            @pl.when(jnp.logical_not(own))
            def _():
                self.copy(row, spot).start()

        loop(0, 8, go)

    def wait_row(self, row):
        def take(t):
            m = row * 8 + t
            pltpu.make_async_copy(self.dst.at[m], self.dst.at[m], self.recv_sem.at[m]).wait()

        loop(0, 8, take)

    def wait_send(self):
        def done(m):
            @pl.when(m != self.me)
            def _():
                self.copy(quo(m, 8), rem(m, 8)).wait_send()

        loop(0, 32, done)


def lane_of(shape):
    return lax.broadcasted_iota(I32, shape, len(shape) - 1)


def pack(column, base=0):
    groups = column.shape[0] // 8
    lane = lane_of((8, 128)) - base
    tile = jnp.zeros((8, 128), F32)
    for g in range(groups):
        tile = jnp.where(lane == g, column[8 * g : 8 * g + 8], tile)
    return tile


def unpack(tile, groups, base=0):
    lane = lane_of((8, 128)) - base
    parts = [jnp.sum(jnp.where(lane == g, tile, 0.0), axis=1, keepdims=True) for g in range(groups)]
    return jnp.concatenate(parts, axis=0)


def pack_slots(column):
    split = column.reshape(8, 3, 8, 1)
    lane = lane_of((8, 8, 128))
    tile = jnp.zeros((8, 8, 128), F32)
    for g in range(3):
        tile = jnp.where(lane == g, split[:, g], tile)
    return tile


def unpack_slots(tile):
    lane = lane_of((8, 8, 128))
    parts = [jnp.sum(jnp.where(lane == g, tile, 0.0), axis=2, keepdims=True)[:, None] for g in range(3)]
    return jnp.concatenate(parts, axis=1).reshape(QD, 1)


def three_parts(column):
    high = column.astype(BF16).astype(F32)
    rest = column - high
    middle = rest.astype(BF16).astype(F32)
    low = rest - middle
    lane = lane_of((column.shape[0], 128))
    parts = jnp.where(lane == 0, high, jnp.where(lane == 1, middle, jnp.where(lane == 2, low, 0.0)))
    return parts.astype(BF16)


def unit(projected):
    length = jnp.sqrt(jnp.sum(projected * projected, axis=1, keepdims=True) + 1e-06)
    return (projected / length).astype(BF16)


def flat(block):
    return block.astype(F32).reshape(block.shape[0] * block.shape[1], EMB)


SCRATCH = dict(
    wq=((2304, EMB), BF16),
    wp=((3072, EMB), BF16),
    hq=((QD, 2304), BF16),
    hp=((QB, 3072), BF16),
    hpool=((512, 3072), BF16),
    q192=((QD, EMB), BF16),
    p48=((QB, EMB), BF16),
    pool=((512, EMB), BF16),
    ids=((8, QD), I32),
    idh=((2, 8, QD), I32),
    qh=((2, 2, QD, EMB), BF16),
    ph=((16, QB, EMB), BF16),
    pp=((QB, EMB), BF16),
    qq=((QB, EMB), BF16),
    pick=((2, 768, QD), BF16),
    xs=((32, SLOTS, EMB), BF16),
    xr=((32, SLOTS, EMB), BF16),
    rs=((32, 8, 128), F32),
    rr=((32, 8, 128), F32),
    e=((768, 768), BF16),
    sums=((8, 128), F32),
    sumr=((16, 8, 128), F32),
    pos=((8, 128), F32),
    posr=((8, 8, 128), F32),
    nq=((768, EMB), F32),
    ns=((384, EMB), BF16),
    nr=((384, EMB), BF16),
    qn=((768, EMB), BF16),
    gs=((768, EMB), BF16),
    gr=((16, QB, EMB), BF16),
    chosen=((768, 512), BF16),
    ys=((32, SLOTS, EMB), BF16),
    yr=((32, SLOTS, EMB), BF16),
    es=((32, 8, 128), F32),
    er=((32, 8, 128), F32),
    tot=((8, 128), F32),
    totl=((8, 8, 128), F32),
    toth=((8, 8, 128), F32),
    invs=((32, 8, 128), F32),
    invr=((32, 8, 128), F32),
    hard=((2, QD, EMB), F32),
    zs=((8, QB, EMB), BF16),
    zr=((8, QB, EMB), BF16),
    pws=((8, 128), F32),
    pwr=((8, 128), F32),
    xw=((768, EMB), BF16),
)
PAIRS = dict(
    ids=2, q=2, p=16, pp=1, qq=1, fwd=2, x=32, r=32, sums=16, pos=8, n=1, y=32, e=32, totl=8, toth=8, inv=32, z=8,
    g=16, pw=1,
)


class Bag:
    pass


def step_kernel(wq, wp, hq, hp, hpool, ids, oq, op, on, *refs):
    v = Bag()
    for name, ref in zip(SCRATCH, refs):
        setattr(v, name, ref)
    rest = refs[len(SCRATCH) :]
    s = {name: (rest[2 * i], rest[2 * i + 1]) for i, name in enumerate(PAIRS)}
    in_sem = rest[2 * len(PAIRS)]
    routes = make_routes()
    y, dp, z, x, c = place()
    line = x * 2 + c
    turn = rem(y + 8 - z, 4)
    lead = quo(z, 4) * 4 + y

    loads = {}
    at = 0
    for name, ref, into, pieces in (
        ("ids", ids, v.ids, 1),
        ("hq", hq, v.hq, 2),
        ("wq", wq, v.wq, 4),
        ("hp", hp, v.hp, 1),
        ("wp", wp, v.wp, 4),
        ("hpool", hpool, v.hpool, 4),
    ):
        size = into.shape[0] // pieces
        loads[name] = []
        for k in range(pieces):
            part = pl.ds(k * size, size)
            loads[name].append(pltpu.make_async_copy(ref.at[part], into.at[part], in_sem.at[at]))
            at += 1
    for group in loads.values():
        for load in group:
            load.start()

    def loaded(*names):
        for name in names:
            for load in loads[name]:
                load.wait()

    barrier = pltpu.get_barrier_semaphore()

    def greet(ty, td):
        pl.semaphore_signal(barrier, inc=1, device_id=(ty, td), device_id_type=MESH)

    wanted = 0
    for name in ("column", "holder", "home", "to_query", "to_passage", "zcore"):
        route = routes[name]
        each(route, lambda i, route=route: greet(*route.source(i)), lambda: None)
        wanted = wanted + route.count - 1
        if route.own is not True:
            wanted = wanted + jnp.where(route.own, 0, 1)

    def greet_plane(i):
        m = rem(y * 8 + line + i, 32)
        greet(quo(m, 8), z * 8 + rem(m, 8))

    loop(1, 32, greet_plane)
    wanted = wanted + 31

    loaded("ids")
    loaded("hq", "wq")
    v.q192[...] = unit(mm(v.hq[...], v.wq[...]))
    own_q = v.q192.at[pl.ds(pl.multiple_of(y * QB, QB), QB), :]
    pl.semaphore_wait(barrier, wanted)
    t_ids = Transfer(routes["column"], lambda i: v.ids, lambda k: v.idh.at[k], s["ids"])
    t_q = Transfer(routes["column"], lambda i: v.q192, lambda k: v.qh.at[c, k], s["q"])
    t_qq = Transfer(routes["to_passage"], lambda i: own_q, lambda k: v.qq, s["qq"])
    t_ids.start()
    t_q.start()
    loaded("hp", "wp")
    v.p48[...] = unit(mm(v.hp[...], v.wp[...]))
    t_p = Transfer(routes["plane_core"], lambda i: v.p48, lambda k: v.ph.at[k], s["p"])
    t_pp = Transfer(routes["to_query"], lambda i: v.p48, lambda k: v.pp, s["pp"])
    t_p.start()
    t_pp.start()
    loaded("hpool")

    def project_pool(i):
        part = pl.ds(pl.multiple_of(i * 256, 256), 256)
        v.pool[part, :] = unit(mm(v.hpool[part, :], v.wp[...]))

    loop(0, 2, project_pool)

    t_ids.wait_recv()
    before = (lax.broadcasted_iota(I32, (QD, QD), 0) < lane_of((QD, QD))).astype(F32).astype(BF16)
    member_row = lax.broadcasted_iota(I32, (32, QD), 0)
    slots, codes = [], []
    for half in range(2):
        held = v.idh[half]
        owner = lax.shift_right_logical(held, 9)
        inside = (lax.shift_right_logical(owner, 3) & 7) == z
        target = jnp.where(inside, lax.shift_right_logical(owner, 6) * 8 + (owner & 7), -1)
        code = ((held & 511) + 1).astype(F32)
        names = [(member_row == target[k : k + 1]).astype(F32) for k in range(8)]
        count = names[0]
        for k in range(1, 8):
            count = count + names[k]
        running = mm(count.astype(BF16), before)
        start = (target * SLOTS + half * CAP).astype(F32)
        rows = []
        for k in range(8):
            rank = jnp.sum(names[k] * running, axis=0, keepdims=True)
            rows.append(jnp.where(target[k : k + 1] >= 0, start[k : k + 1] + rank, -1.0))
            running = running + names[k]
        slots.append(rows)
        codes.append([code[k : k + 1] for k in range(8)])

    def forward(k):
        return pltpu.make_async_remote_copy(
            src_ref=v.qh.at[c, k],
            dst_ref=v.qh.at[c, k],
            send_sem=s["fwd"][0].at[k],
            recv_sem=s["fwd"][1].at[k],
            device_id=(y, dp + 1 - 2 * c),
            device_id_type=MESH,
        )

    def hand_on(k):
        t_q.wait_slot(k)
        forward(k).start()

    loop(0, 2, hand_on)

    t_x = PlaneTransfer(v.xs, v.xr, s["x"])
    t_r = PlaneTransfer(v.rs, v.rr, s["r"])

    def ask(j):
        row = rem(y + j, 4)
        here = pl.ds(pl.multiple_of(row * QD, QD), QD)
        spot = (lax.broadcasted_iota(I32, (QD, QD), 0) + row * QD).astype(F32)
        found = jnp.zeros((QD, QD), F32)
        asked = jnp.zeros((QD, EMB), F32)
        for half in range(2):
            hits = jnp.zeros((QD, QD), F32)
            for k in range(8):
                hits = jnp.where(spot == slots[half][k], codes[half][k], hits)
            found = found + hits
            picked = jnp.where(hits > 0.0, 1.0, 0.0).astype(BF16)
            v.pick[half, here, :] = picked
            asked = asked + mm(picked, v.qh[c, half])
        v.xs[pl.ds(row * 8, 8)] = asked.reshape(8, SLOTS, EMB).astype(BF16)
        v.rs[pl.ds(row * 8, 8)] = pack_slots(jnp.sum(found, axis=1, keepdims=True))
        t_r.start_row(row)
        t_x.start_row(row)

    loop(0, 4, ask)

    t_pp.wait_recv()
    pos_exp = jnp.exp(logit_scale * jnp.sum(own_q[...].astype(F32) * v.pp[...].astype(F32), axis=1, keepdims=True))
    v.pos[...] = pack(pos_exp, lead * 6)
    t_pos = Transfer(routes["holder"], lambda i: v.pos, lambda k: v.posr.at[k], s["pos"])
    t_pos.start()

    t_p.wait_recv()

    def taken(k):
        pltpu.make_async_copy(v.qh.at[1 - c, k], v.qh.at[1 - c, k], s["fwd"][1].at[k]).wait()

    loop(0, 2, taken)

    def queries(j):
        return v.qh[quo(j, 2), rem(j, 2)]

    def score(j, tile):
        here = pl.ds(pl.multiple_of(j * QD, QD), QD)
        passages = v.ph[...].reshape(768, EMB)
        grown = jnp.exp(logit_scale * mm(queries(j), passages, NT))
        low = grown.astype(BF16)
        v.e[here, :] = low
        v.nq[here, :] = mm(low, passages)
        return tile + pack(jnp.sum(grown, axis=1, keepdims=True), j * 24)

    v.sums[...] = lax.fori_loop(0, 4, score, jnp.zeros((8, 128), F32))
    t_sums = Transfer(routes["zcore"], lambda i: v.sums, lambda k: v.sumr.at[k], s["sums"])
    t_sums.start()
    v.ns[...] = v.nq[pl.ds(pl.multiple_of((1 - c) * 384, 384), 384), :].astype(BF16)
    send_n = pltpu.make_async_remote_copy(
        src_ref=v.ns,
        dst_ref=v.nr,
        send_sem=s["n"][0].at[0],
        recv_sem=s["n"][1].at[0],
        device_id=(y, dp + 1 - 2 * c),
        device_id_type=MESH,
    )
    send_n.start()
    t_sums.wait_recv()
    inv_batch = 1.0 / jnp.where(lane_of((8, 128)) < 96, jnp.sum(v.sumr[...], axis=0), 1.0)

    def scale_queries(j):
        here = pl.ds(pl.multiple_of(j * QD, QD), QD)
        v.qn[here, :] = (queries(j).astype(F32) * unpack(inv_batch, 24, j * 24)).astype(BF16)

    loop(0, 4, scale_queries)
    for j in range(3):
        v.gs[256 * j : 256 * j + 256, :] = mm(v.e[:, 256 * j : 256 * j + 256], v.qn[...], TN).astype(BF16)

    t_y = PlaneTransfer(v.ys, v.yr, s["y"])
    t_e = PlaneTransfer(v.es, v.er, s["e"])

    def answer(j):
        row = rem(y + 4 - j, 4)
        here = pl.ds(pl.multiple_of(row * QD, QD), QD)
        t_r.wait_row(row)
        t_x.wait_row(row)
        code = unpack_slots(v.rr[pl.ds(row * 8, 8)])
        chosen = jnp.where(code == (lane_of((QD, 512)) + 1).astype(F32), 1.0, 0.0).astype(BF16)
        v.chosen[here, :] = chosen
        named = mm(chosen, v.pool[...])
        asked = flat(v.xr[pl.ds(row * 8, 8)])
        neg_exp = jnp.exp(logit_scale * jnp.sum(asked * named, axis=1, keepdims=True))
        v.es[pl.ds(row * 8, 8)] = pack_slots(neg_exp)
        t_e.start_row(row)
        v.ys[pl.ds(row * 8, 8)] = (neg_exp * named).reshape(8, SLOTS, EMB).astype(BF16)
        t_y.start_row(row)

    loop(0, 4, answer)
    t_qq.start()

    def total(j, carry):
        row = rem(y + j, 4)
        here = pl.ds(pl.multiple_of(row * QD, QD), QD)
        t_e.wait_row(row)
        parts = three_parts(unpack_slots(v.er[pl.ds(row * 8, 8)]))
        return tuple(carry[half] + mm(v.pick[half, here, :], parts, TN) for half in range(2))

    both = lax.fori_loop(0, 4, total, (jnp.zeros((QD, 128), F32), jnp.zeros((QD, 128), F32)))
    column = jnp.concatenate([jnp.sum(t, axis=1, keepdims=True) for t in both], axis=0)
    v.tot[...] = pack(column)
    t_totl = Transfer(routes["zline"], lambda i: v.tot, lambda k: v.totl.at[k], s["totl"])
    t_toth = Transfer(routes["home"], lambda i: v.tot, lambda k: v.toth.at[k], s["toth"])
    t_totl.start()
    t_toth.start()
    t_y.wait_send()
    core = routes["plane_core"]
    t_g = Transfer(
        core,
        lambda i: v.gs.at[pl.ds(pl.multiple_of(core.item(i) * QB, QB), QB), :],
        lambda k: v.gr.at[k],
        s["g"],
    )
    t_g.start()
    t_pos.wait_recv()
    t_totl.wait_recv()
    hard_total = jnp.sum(v.totl[...], axis=0) + jnp.sum(v.posr[...], axis=0)
    inv_hard_tile = 1.0 / jnp.where(lane_of((8, 128)) < 48, hard_total, 1.0)
    inv_hard = [unpack(inv_hard_tile, 24, 24 * half) for half in range(2)]
    inv_parts = [three_parts(inv_hard[half]) for half in range(2)]
    t_inv = PlaneTransfer(v.invs, v.invr, s["inv"])

    def tell(j):
        row = rem(y + j, 4)
        here = pl.ds(pl.multiple_of(row * QD, QD), QD)
        shares = mm(v.pick[0, here, :], inv_parts[0]) + mm(v.pick[1, here, :], inv_parts[1])
        v.invs[pl.ds(row * 8, 8)] = pack_slots(jnp.sum(shares, axis=1, keepdims=True))
        t_inv.start_row(row)

    loop(0, 4, tell)
    t_toth.wait_recv()
    own_total = unpack(jnp.sum(v.toth[...], axis=0), 6, lead * 6)
    pos_coef = pos_exp / (pos_exp + own_total) - 2.0
    v.pws[...] = pack(pos_coef)
    t_pw = Transfer(routes["to_passage"], lambda i: v.pws, lambda k: v.pwr, s["pw"])
    t_pw.start()

    v.hard[...] = jnp.zeros((2, QD, EMB), F32)

    def collect(j):
        row = rem(y + j, 4)
        here = pl.ds(pl.multiple_of(row * QD, QD), QD)
        t_y.wait_row(row)
        rows = flat(v.yr[pl.ds(row * 8, 8)]).astype(BF16)
        for half in range(2):
            v.hard[half] += mm(v.pick[half, here, :], rows, TN)

    loop(0, 4, collect)
    pltpu.make_async_copy(v.nr, v.nr, s["n"][1].at[0]).wait()
    t_z = Transfer(routes["home"], lambda i: v.zs.at[routes["home"].item(i)], lambda k: v.zr.at[k], s["z"])
    for half in range(2):
        mine = v.nq[pl.ds(pl.multiple_of(c * 384 + half * QD, QD), QD), :] + v.nr[half * QD : half * QD + QD, :].astype(F32)
        inv_own = unpack(inv_batch, 24, c * 48 + half * 24)
        mixed = mine * inv_own + v.hard[half] * inv_hard[half]
        v.zs[4 * half : 4 * half + 4] = mixed.astype(BF16).reshape(4, QB, EMB)
    t_z.start()
    def weigh(j):
        row = rem(y + 4 - j, 4)
        here = pl.ds(pl.multiple_of(row * QD, QD), QD)
        t_inv.wait_row(row)
        share = unpack_slots(v.es[pl.ds(row * 8, 8)]) * unpack_slots(v.invr[pl.ds(row * 8, 8)])
        v.xw[here, :] = (flat(v.xr[pl.ds(row * 8, 8)]) * share).astype(BF16)

    loop(0, 4, weigh)
    for j in range(2):
        part = mm(v.chosen[:, 256 * j : 256 * j + 256], v.xw[...], TN)
        on[256 * j : 256 * j + 256, :] = (logit_scale * part).astype(BF16)

    t_z.wait_recv()
    summed = jnp.sum(v.zr[...].astype(F32), axis=0)
    oq[...] = (logit_scale * (summed + pos_coef * v.pp[...].astype(F32))).astype(BF16)
    t_pw.wait_recv()
    t_qq.wait_recv()
    t_g.wait_recv()
    summed = jnp.sum(v.gr[...].astype(F32), axis=0)
    coef = unpack(v.pwr[...], 6)
    op[...] = (logit_scale * (summed + coef * v.qq[...].astype(F32))).astype(BF16)

    for t in (t_ids, t_q, t_qq, t_pp, t_p, t_r, t_x, t_pos, t_sums, t_e, t_totl, t_toth, t_inv, t_pw, t_z, t_g):
        t.wait_send()
    loop(0, 2, lambda k: forward(k).wait_send())
    send_n.wait_send()


def settle_kernel(q, p, n, oq, op, on):
    oq[...] = q[...]
    op[...] = p[...]
    on[...] = n[...]


def shards(query_hidden, passage_hidden, pool_hidden, query_proj, passage_proj, negative_ids):
    scratch = [pltpu.VMEM(shape, dtype) for shape, dtype in SCRATCH.values()]
    for n in PAIRS.values():
        scratch += [pltpu.SemaphoreType.DMA((n,)), pltpu.SemaphoreType.DMA((n,))]
    scratch.append(pltpu.SemaphoreType.DMA((16,)))
    results = pl.pallas_call(
        step_kernel,
        out_shape=[jax.ShapeDtypeStruct((n, EMB), BF16) for n in (QB, QB, 512)],
        in_specs=[pl.BlockSpec(memory_space=pl.ANY)] * 6,
        out_specs=[pl.BlockSpec(memory_space=pltpu.VMEM)] * 3,
        scratch_shapes=scratch,
        compiler_params=pltpu.CompilerParams(
            collective_id=1, has_side_effects=True, vmem_limit_bytes=60 * 1024 * 1024
        ),
        name="contrastive_step",
    )(query_proj, passage_proj, query_hidden, passage_hidden, pool_hidden, negative_ids.T)
    return pl.pallas_call(
        settle_kernel,
        out_shape=[jax.ShapeDtypeStruct((n, EMB), BF16) for n in (QB, QB, 512)],
        in_specs=[pl.BlockSpec(memory_space=pltpu.VMEM)] * 3,
        out_specs=[pl.BlockSpec(memory_space=pltpu.VMEM)] * 3,
        name="settle",
    )(*results)


def solution(mesh):
    placed = (
        P("dp", None),
        P(("tower", "dp"), None),
        P(("tower", "dp"), None),
        P(),
        P(),
        P("dp", None),
    )
    return jax.shard_map(
        shards,
        mesh=mesh,
        in_specs=placed,
        out_specs=(P(("dp", "tower"), None), P(("tower", "dp"), None), P(("tower", "dp"), None)),
        check_vma=False,
    )
```

```python
import jax
import jax.numpy as jnp
from jax import lax
from jax.experimental import pallas as pl
from jax.experimental.pallas import tpu as pltpu
from jax.sharding import PartitionSpec as P

logit_scale = 50.0
MESH = pl.DeviceIdType.MESH
F32 = jnp.float32
BF16 = jnp.bfloat16
I32 = jnp.int32
EMB = 768
CAP = 12
SLOTS = 2 * CAP
QB = 48
QD = 192
NN = (((1,), (0,)), ((), ()))
NT = (((1,), (1,)), ((), ()))
TN = (((0,), (0,)), ((), ()))


def mm(a, b, dims=NN):
    return lax.dot_general(a, b, dims, preferred_element_type=F32)


def rem(a, n):
    return lax.rem(a, n)


def quo(a, n):
    return lax.div(a, n)


def loop(lo, hi, body):
    def step(i, carry):
        body(i)
        return carry

    lax.fori_loop(lo, hi, step, 0)


def place():
    y = lax.axis_index("tower")
    dp = lax.axis_index("dp")
    return y, dp, quo(dp, 8), rem(quo(dp, 2), 4), rem(dp, 2)


class Route:
    def __init__(self, count, dest, source, slot, own, item=None):
        self.count, self.dest, self.source = count, dest, source
        self.slot, self.own, self.item = slot, own, item


def make_routes():
    y, dp, z, x, c = place()
    line = x * 2 + c
    turn = rem(y + 8 - z, 4)
    lead = quo(z, 4) * 4 + y
    at_home = rem(2 * z, 4) == y

    def plane_core(i):
        n = rem(y * 4 + x + i, 16)
        return quo(n, 4), z * 8 + rem(n, 4) * 2 + c

    def zcore(i):
        g = rem(z * 2 + c + i, 16)
        zz = quo(g, 2)
        return rem(turn + zz, 4), zz * 8 + x * 2 + rem(g, 2)

    def zline(i):
        zz = rem(z + i, 8)
        return rem(turn + zz, 4), zz * 8 + line

    def holder(i):
        zz = rem(z + i, 8)
        return rem(z + zz, 4), zz * 8 + line

    def column(i):
        return y, (turn + 4 * rem(quo(z, 4) + i, 2)) * 8 + line

    def home(i):
        k = rem(lead + i, 8)
        return rem(k, 4), (turn + 4 * quo(k, 4)) * 8 + line

    to_query = (rem(dp, 4), y * 16 + quo(dp, 4))
    to_passage = (quo(dp, 16), rem(dp, 16) * 4 + y)
    query_own = (to_query[0] == y) & (to_query[1] == dp)
    passage_own = (to_passage[0] == y) & (to_passage[1] == dp)
    return {
        "plane_core": Route(16, plane_core, plane_core, y * 4 + x, True, lambda i: rem(y * 4 + x + i, 16)),
        "zline": Route(8, zline, zline, z, True),
        "zcore": Route(16, zcore, zcore, z * 2 + c, True),
        "column": Route(2, column, column, quo(z, 4), at_home),
        "holder": Route(8, holder, home, lead, at_home),
        "home": Route(8, home, holder, z, at_home, lambda i: rem(lead + i, 8)),
        "to_query": Route(1, lambda i: to_query, lambda i: to_passage, 0, query_own),
        "to_passage": Route(1, lambda i: to_passage, lambda i: to_query, 0, passage_own),
    }


def each(route, far, near):
    if route.own is True:
        near()
    else:

        @pl.when(route.own)
        def _():
            near()

        @pl.when(jnp.logical_not(route.own))
        def _():
            far(0)

    if route.count > 1:
        loop(1, route.count, far)


class Transfer:
    def __init__(self, route, src, into, sems):
        self.route, self.src, self.into = route, src, into
        self.send_sem, self.recv_sem = sems[0].at[0], sems[1].at[0]

    def spot(self):
        return self.into if self.route.count == 1 else self.into.at[self.route.slot]

    def copy(self, i):
        return pltpu.make_async_remote_copy(
            src_ref=self.src(i),
            dst_ref=self.spot(),
            send_sem=self.send_sem,
            recv_sem=self.recv_sem,
            device_id=self.route.dest(i),
            device_id_type=MESH,
        )

    def local(self):
        return pltpu.make_async_copy(self.src(0), self.spot(), self.recv_sem)

    def start(self):
        each(self.route, lambda i: self.copy(i).start(), lambda: self.local().start())

    def wait_recv(self):
        pltpu.make_async_copy(self.into, self.into, self.recv_sem).wait()

    def wait_send(self):
        def taken(n):
            part = self.into if n == self.route.count else self.into.at[pl.ds(0, n)]
            pltpu.make_async_copy(part, part, self.send_sem).wait()

        n = self.route.count
        if self.route.own is True:
            taken(n - 1)
        else:
            if n > 1:

                @pl.when(self.route.own)
                def _():
                    taken(n - 1)

            @pl.when(jnp.logical_not(self.route.own))
            def _():
                taken(n)


class PlaneTransfer:
    def __init__(self, src, dst, sems, spots):
        self.src, self.dst, self.spots = src, dst, spots
        self.send_sem, self.recv_sem = sems[0].at[0], sems[1]
        y, dp, z, x, c = place()
        self.y, self.base, self.me = y, z * 8, y * 8 + x * 2 + c

    def start_row(self, row, first):
        def far(spot):
            pltpu.make_async_remote_copy(
                src_ref=self.src.at[row * 8 + spot],
                dst_ref=self.dst.at[self.me],
                send_sem=self.send_sem,
                recv_sem=self.recv_sem.at[self.y],
                device_id=(row, self.base + spot),
                device_id_type=MESH,
            ).start()

        def near():
            pltpu.make_async_copy(self.src.at[self.me], self.dst.at[self.me], self.recv_sem.at[self.y]).start()

        if isinstance(first, bool):
            near() if first else far(self.spots[0])
        else:
            pl.when(first)(near)
            pl.when(jnp.logical_not(first))(lambda: far(self.spots[0]))

        for spot in self.spots[1:]:
            far(spot)

    def wait_row(self, row):
        part = self.dst.at[pl.ds(row * 8, 8)]
        pltpu.make_async_copy(part, part, self.recv_sem.at[row]).wait()

    def wait_send(self):
        part = self.src.at[pl.ds(0, 31)]
        pltpu.make_async_copy(part, part, self.send_sem).wait()


def lane_of(shape):
    return lax.broadcasted_iota(I32, shape, len(shape) - 1)


def pack(column, base=0):
    groups = column.shape[0] // 8
    lane = lane_of((8, 128)) - base
    tile = jnp.zeros((8, 128), F32)
    for g in range(groups):
        tile = jnp.where(lane == g, column[8 * g : 8 * g + 8], tile)
    return tile


def unpack(tile, groups, base=0):
    lane = lane_of((8, 128)) - base
    parts = [jnp.sum(jnp.where(lane == g, tile, 0.0), axis=1, keepdims=True) for g in range(groups)]
    return jnp.concatenate(parts, axis=0)


def pack_slots(column):
    split = column.reshape(8, 3, 8, 1)
    lane = lane_of((8, 8, 128))
    tile = jnp.zeros((8, 8, 128), F32)
    for g in range(3):
        tile = jnp.where(lane == g, split[:, g], tile)
    return tile


def unpack_slots(tile):
    lane = lane_of((8, 8, 128))
    parts = [jnp.sum(jnp.where(lane == g, tile, 0.0), axis=2, keepdims=True)[:, None] for g in range(3)]
    return jnp.concatenate(parts, axis=1).reshape(QD, 1)


def three_parts(column):
    high = column.astype(BF16).astype(F32)
    rest = column - high
    middle = rest.astype(BF16).astype(F32)
    low = rest - middle
    lane = lane_of((column.shape[0], 128))
    parts = jnp.where(lane == 0, high, jnp.where(lane == 1, middle, jnp.where(lane == 2, low, 0.0)))
    return parts.astype(BF16)


def unit(projected):
    length = jnp.sqrt(jnp.sum(projected * projected, axis=1, keepdims=True) + 1e-06)
    return (projected / length).astype(BF16)


def flat(block):
    return block.astype(F32).reshape(block.shape[0] * block.shape[1], EMB)


SCRATCH = dict(
    wq=((2304, EMB), BF16),
    wp=((3072, EMB), BF16),
    hq=((QD, 2304), BF16),
    hp=((QB, 3072), BF16),
    hpool=((512, 3072), BF16),
    q192=((QD, EMB), BF16),
    p48=((QB, EMB), BF16),
    pool=((512, EMB), BF16),
    ids=((8, QD), I32),
    idh=((2, 8, QD), I32),
    qh=((2, 2, QD, EMB), BF16),
    ph=((16, QB, EMB), BF16),
    pp=((QB, EMB), BF16),
    qq=((QB, EMB), BF16),
    pick=((2, 768, QD), BF16),
    xs=((32, SLOTS, EMB), BF16),
    xr=((32, SLOTS, EMB), BF16),
    rs=((32, 8, 128), F32),
    rr=((32, 8, 128), F32),
    e=((768, 768), BF16),
    sums=((8, 128), F32),
    sumr=((16, 8, 128), F32),
    pos=((8, 128), F32),
    posr=((8, 8, 128), F32),
    nq=((768, EMB), F32),
    ns=((384, EMB), BF16),
    nr=((384, EMB), BF16),
    qn=((768, EMB), BF16),
    gs=((768, EMB), BF16),
    gr=((16, QB, EMB), BF16),
    chosen=((768, 512), BF16),
    ys=((2, 32, SLOTS, EMB // 2), BF16),
    yr=((2, 32, SLOTS, EMB // 2), BF16),
    es=((32, 8, 128), F32),
    er=((32, 8, 128), F32),
    tot=((8, 128), F32),
    totl=((8, 8, 128), F32),
    toth=((8, 8, 128), F32),
    invs=((32, 8, 128), F32),
    invr=((32, 8, 128), F32),
    hard=((2, QD, EMB), F32),
    zs=((2, 8, QB, EMB // 2), BF16),
    zr=((2, 8, QB, EMB // 2), BF16),
    pws=((8, 128), F32),
    pwr=((8, 128), F32),
    xw=((768, EMB), BF16),
)
PAIRS = dict(
    ids=1, q=1, p=1, pp=1, qq=1, fwd=2, x=4, r=4, sums=1, pos=1, n=1, y=4, y1=4, e=4, totl=1, toth=1, inv=4, z=1, z1=1, g=1, pw=1
)


class Bag:
    pass


def step_kernel(wq, wp, hq, hp, hpool, ids, oq, op, on, *refs):
    v = Bag()
    for name, ref in zip(SCRATCH, refs):
        setattr(v, name, ref)
    rest = refs[len(SCRATCH) :]
    s = {name: (rest[2 * i], rest[2 * i + 1]) for i, name in enumerate(PAIRS)}
    in_sem = rest[2 * len(PAIRS)]
    routes = make_routes()
    y, dp, z, x, c = place()
    line = x * 2 + c
    turn = rem(y + 8 - z, 4)
    lead = quo(z, 4) * 4 + y

    loads = {}
    at = 0
    for name, ref, into, pieces in (
        ("ids", ids, v.ids, 1),
        ("hq", hq, v.hq, 2),
        ("wq", wq, v.wq, 4),
        ("hp", hp, v.hp, 1),
        ("wp", wp, v.wp, 4),
        ("hpool", hpool, v.hpool, 4),
    ):
        size = into.shape[0] // pieces
        loads[name] = []
        for k in range(pieces):
            part = pl.ds(k * size, size)
            loads[name].append(pltpu.make_async_copy(ref.at[part], into.at[part], in_sem.at[at]))
            at += 1

    def fetch(*names):
        for name in names:
            for load in loads[name]:
                load.start()

    fetch("ids", "hq", "wq")

    def loaded(*names):
        for name in names:
            for load in loads[name]:
                load.wait()

    barrier = pltpu.get_barrier_semaphore()

    def greet(ty, td):
        pl.semaphore_signal(barrier, inc=1, device_id=(ty, td), device_id_type=MESH)

    wanted = 0
    for name in ("column", "holder", "home", "to_query", "to_passage", "zcore"):
        route = routes[name]
        each(route, lambda i, route=route: greet(*route.source(i)), lambda: None)
        wanted = wanted + route.count - 1
        if route.own is not True:
            wanted = wanted + jnp.where(route.own, 0, 1)

    def greet_plane(i):
        m = rem(y * 8 + line + i, 32)
        greet(quo(m, 8), z * 8 + rem(m, 8))

    loop(1, 32, greet_plane)
    wanted = wanted + 31

    fetch("hp", "wp")
    loaded("ids", "hq", "wq")
    fetch("hpool")
    v.q192[...] = unit(mm(v.hq[...], v.wq[...]))
    own_q = v.q192.at[pl.ds(pl.multiple_of(y * QB, QB), QB), :]
    pl.semaphore_wait(barrier, wanted)
    t_ids = Transfer(routes["column"], lambda i: v.ids, v.idh, s["ids"])
    t_q = Transfer(routes["column"], lambda i: v.q192, v.qh.at[c], s["q"])
    t_qq = Transfer(routes["to_passage"], lambda i: own_q, v.qq, s["qq"])
    t_ids.start()
    t_q.start()
    loaded("hp", "wp")
    v.p48[...] = unit(mm(v.hp[...], v.wp[...]))
    t_p = Transfer(routes["plane_core"], lambda i: v.p48, v.ph, s["p"])
    t_pp = Transfer(routes["to_query"], lambda i: v.p48, v.pp, s["pp"])
    t_p.start()
    loaded("hpool")

    def project_pool(i):
        part = pl.ds(pl.multiple_of(i * 256, 256), 256)
        v.pool[part, :] = unit(mm(v.hpool[part, :], v.wp[...]))

    loop(0, 2, project_pool)

    t_ids.wait_recv()
    before = (lax.broadcasted_iota(I32, (QD, QD), 0) < lane_of((QD, QD))).astype(F32).astype(BF16)
    member_row = lax.broadcasted_iota(I32, (32, QD), 0)
    slots, codes = [], []
    for half in range(2):
        held = v.idh[half]
        owner = lax.shift_right_logical(held, 9)
        inside = (lax.shift_right_logical(owner, 3) & 7) == z
        target = jnp.where(inside, lax.shift_right_logical(owner, 6) * 8 + (owner & 7), -1)
        code = ((held & 511) + 1).astype(F32)
        names = [(member_row == target[k : k + 1]).astype(F32) for k in range(8)]
        count = names[0]
        for k in range(1, 8):
            count = count + names[k]
        running = mm(count.astype(BF16), before)
        start = (target * SLOTS + half * CAP).astype(F32)
        rows = []
        for k in range(8):
            rank = jnp.sum(names[k] * running, axis=0, keepdims=True)
            rows.append(jnp.where(target[k : k + 1] >= 0, start[k : k + 1] + rank, -1.0))
            running = running + names[k]
        slots.append(rows)
        codes.append([code[k : k + 1] for k in range(8)])

    def forward(k):
        return pltpu.make_async_remote_copy(
            src_ref=v.qh.at[c, k],
            dst_ref=v.qh.at[c, k],
            send_sem=s["fwd"][0].at[k],
            recv_sem=s["fwd"][1].at[k],
            device_id=(y, dp + 1 - 2 * c),
            device_id_type=MESH,
        )

    t_q.wait_recv()
    forward(0).start()
    forward(1).start()

    spots = [rem(line + t, 8) for t in range(8)]
    t_x = PlaneTransfer(v.xs, v.xr, s["x"], spots)
    t_r = PlaneTransfer(v.rs, v.rr, s["r"], spots)

    def ask(j):
        row = rem(y + j, 4)
        here = pl.ds(pl.multiple_of(row * QD, QD), QD)
        spot = (lax.broadcasted_iota(I32, (QD, QD), 0) + row * QD).astype(F32)
        found = jnp.zeros((QD, QD), F32)
        asked = jnp.zeros((QD, EMB), F32)
        for half in range(2):
            hits = jnp.zeros((QD, QD), F32)
            for k in range(8):
                hits = jnp.where(spot == slots[half][k], codes[half][k], hits)
            found = found + hits
            picked = jnp.where(hits > 0.0, 1.0, 0.0).astype(BF16)
            v.pick[half, here, :] = picked
            asked = asked + mm(picked, v.qh[c, half])
        v.xs[pl.ds(row * 8, 8)] = asked.reshape(8, SLOTS, EMB).astype(BF16)
        v.rs[pl.ds(row * 8, 8)] = pack_slots(jnp.sum(found, axis=1, keepdims=True))
        t_r.start_row(row, j == 0)
        t_x.start_row(row, j == 0)

    loop(0, 4, ask)

    t_pp.start()

    t_p.wait_recv()

    def taken(k):
        pltpu.make_async_copy(v.qh.at[1 - c, k], v.qh.at[1 - c, k], s["fwd"][1].at[k]).wait()

    taken(0)
    taken(1)

    def queries(j):
        return v.qh[quo(j, 2), rem(j, 2)]

    def score(j, tile):
        here = pl.ds(pl.multiple_of(j * QD, QD), QD)
        passages = v.ph[...].reshape(768, EMB)
        grown = jnp.exp(logit_scale * mm(queries(j), passages, NT))
        low = grown.astype(BF16)
        v.e[here, :] = low
        v.nq[here, :] = mm(low, passages)
        return tile + pack(jnp.sum(grown, axis=1, keepdims=True), j * 24)

    v.sums[...] = lax.fori_loop(0, 4, score, jnp.zeros((8, 128), F32))
    t_sums = Transfer(routes["zcore"], lambda i: v.sums, v.sumr, s["sums"])
    t_sums.start()
    v.ns[...] = v.nq[pl.ds(pl.multiple_of((1 - c) * 384, 384), 384), :].astype(BF16)
    send_n = pltpu.make_async_remote_copy(
        src_ref=v.ns,
        dst_ref=v.nr,
        send_sem=s["n"][0].at[0],
        recv_sem=s["n"][1].at[0],
        device_id=(y, dp + 1 - 2 * c),
        device_id_type=MESH,
    )
    send_n.start()
    t_sums.wait_recv()
    inv_batch = 1.0 / jnp.where(lane_of((8, 128)) < 96, jnp.sum(v.sumr[...], axis=0), 1.0)

    def scale_queries(j):
        here = pl.ds(pl.multiple_of(j * QD, QD), QD)
        v.qn[here, :] = (queries(j).astype(F32) * unpack(inv_batch, 24, j * 24)).astype(BF16)

    loop(0, 4, scale_queries)
    for j in range(3):
        v.gs[256 * j : 256 * j + 256, :] = mm(v.e[:, 256 * j : 256 * j + 256], v.qn[...], TN).astype(BF16)

    t_y = [PlaneTransfer(v.ys.at[h], v.yr.at[h], s[name], spots) for h, name in enumerate(("y", "y1"))]
    t_e = PlaneTransfer(v.es, v.er, s["e"], spots)

    def answer(j):
        row = rem(y + 4 - j, 4)
        here = pl.ds(pl.multiple_of(row * QD, QD), QD)
        t_r.wait_row(row)
        t_x.wait_row(row)
        code = unpack_slots(v.rr[pl.ds(row * 8, 8)])
        chosen = jnp.where(code == (lane_of((QD, 512)) + 1).astype(F32), 1.0, 0.0).astype(BF16)
        v.chosen[here, :] = chosen
        named = mm(chosen, v.pool[...])
        asked = flat(v.xr[pl.ds(row * 8, 8)])
        neg_exp = jnp.exp(logit_scale * jnp.sum(asked * named, axis=1, keepdims=True))
        v.es[pl.ds(row * 8, 8)] = pack_slots(neg_exp)
        t_e.start_row(row, j == 0)
        rows = (neg_exp * named).reshape(8, SLOTS, EMB).astype(BF16)
        for h in range(2):
            v.ys[h, pl.ds(row * 8, 8)] = rows[:, :, 384 * h : 384 * h + 384]

    loop(0, 4, answer)
    t_qq.start()

    def give(h, j):
        t_y[h].start_row(rem(y + 4 - j, 4), j == 0)

    give(0, 0)

    t_pp.wait_recv()
    pos_exp = jnp.exp(logit_scale * jnp.sum(own_q[...].astype(F32) * v.pp[...].astype(F32), axis=1, keepdims=True))
    v.pos[...] = pack(pos_exp, lead * 6)
    t_pos = Transfer(routes["holder"], lambda i: v.pos, v.posr, s["pos"])
    t_pos.start()

    def total(j, carry):
        row = rem(y + j, 4)
        here = pl.ds(pl.multiple_of(row * QD, QD), QD)
        t_e.wait_row(row)
        parts = three_parts(unpack_slots(v.er[pl.ds(row * 8, 8)]))
        return tuple(carry[half] + mm(v.pick[half, here, :], parts, TN) for half in range(2))

    both = lax.fori_loop(0, 4, total, (jnp.zeros((QD, 128), F32), jnp.zeros((QD, 128), F32)))
    column = jnp.concatenate([jnp.sum(t, axis=1, keepdims=True) for t in both], axis=0)
    v.tot[...] = pack(column)
    t_totl = Transfer(routes["zline"], lambda i: v.tot, v.totl, s["totl"])
    t_toth = Transfer(routes["home"], lambda i: v.tot, v.toth, s["toth"])
    t_totl.start()
    t_toth.start()
    loop(1, 4, lambda j: give(0, j))
    loop(0, 4, lambda j: give(1, j))
    t_pos.wait_recv()
    t_totl.wait_recv()
    hard_total = jnp.sum(v.totl[...], axis=0) + jnp.sum(v.posr[...], axis=0)
    inv_hard_tile = 1.0 / jnp.where(lane_of((8, 128)) < 48, hard_total, 1.0)
    inv_hard = [unpack(inv_hard_tile, 24, 24 * half) for half in range(2)]
    inv_parts = [three_parts(inv_hard[half]) for half in range(2)]
    t_inv = PlaneTransfer(v.invs, v.invr, s["inv"], spots)

    def tell(j):
        row = rem(y + j, 4)
        here = pl.ds(pl.multiple_of(row * QD, QD), QD)
        shares = mm(v.pick[0, here, :], inv_parts[0]) + mm(v.pick[1, here, :], inv_parts[1])
        v.invs[pl.ds(row * 8, 8)] = pack_slots(jnp.sum(shares, axis=1, keepdims=True))
        t_inv.start_row(row, j == 0)

    loop(0, 4, tell)
    t_toth.wait_recv()
    own_total = unpack(jnp.sum(v.toth[...], axis=0), 6, lead * 6)
    pos_coef = pos_exp / (pos_exp + own_total) - 2.0
    v.pws[...] = pack(pos_coef)
    t_pw = Transfer(routes["to_passage"], lambda i: v.pws, v.pwr, s["pw"])
    t_pw.start()

    v.hard[...] = jnp.zeros((2, QD, EMB), F32)

    def collect(h):
        lanes = slice(384 * h, 384 * h + 384)

        def gather(j):
            row = rem(y + j, 4)
            here = pl.ds(pl.multiple_of(row * QD, QD), QD)
            t_y[h].wait_row(row)
            rows = v.yr[h, pl.ds(row * 8, 8)].astype(F32).reshape(QD, 384).astype(BF16)
            for half in range(2):
                v.hard[half, :, lanes] += mm(v.pick[half, here, :], rows, TN)

        loop(0, 4, gather)
        for half in range(2):
            own = v.nq[pl.ds(pl.multiple_of(c * 384 + half * QD, QD), QD), lanes]
            mine = own + v.nr[half * QD : half * QD + QD, lanes].astype(F32)
            inv_own = unpack(inv_batch, 24, c * 48 + half * 24)
            mixed = mine * inv_own + v.hard[half, :, lanes] * inv_hard[half]
            v.zs[h, 4 * half : 4 * half + 4] = mixed.astype(BF16).reshape(4, QB, 384)

    home = routes["home"]
    t_z = [
        Transfer(home, lambda i, h=h: v.zs.at[h, home.item(i)], v.zr.at[h], s[name])
        for h, name in enumerate(("z", "z1"))
    ]
    pltpu.make_async_copy(v.nr, v.nr, s["n"][1].at[0]).wait()
    collect(0)
    t_z[0].start()
    core = routes["plane_core"]
    t_g = Transfer(
        core,
        lambda i: v.gs.at[pl.ds(pl.multiple_of(core.item(i) * QB, QB), QB), :],
        v.gr,
        s["g"],
    )
    t_g.start()
    collect(1)
    t_z[1].start()

    def weigh(j):
        row = rem(y + 4 - j, 4)
        here = pl.ds(pl.multiple_of(row * QD, QD), QD)
        t_inv.wait_row(row)
        share = unpack_slots(v.es[pl.ds(row * 8, 8)]) * unpack_slots(v.invr[pl.ds(row * 8, 8)])
        v.xw[here, :] = (flat(v.xr[pl.ds(row * 8, 8)]) * share).astype(BF16)

    loop(0, 4, weigh)
    for j in range(2):
        part = mm(v.chosen[:, 256 * j : 256 * j + 256], v.xw[...], TN)
        on[256 * j : 256 * j + 256, :] = (logit_scale * part).astype(BF16)

    for h in range(2):
        t_z[h].wait_recv()
        lanes = slice(384 * h, 384 * h + 384)
        summed = jnp.sum(v.zr[h].astype(F32), axis=0)
        oq[:, lanes] = (logit_scale * (summed + pos_coef * v.pp[:, lanes].astype(F32))).astype(BF16)
    t_pw.wait_recv()
    t_qq.wait_recv()
    t_g.wait_recv()
    summed = jnp.sum(v.gr[...].astype(F32), axis=0)
    coef = unpack(v.pwr[...], 6)
    op[...] = (logit_scale * (summed + coef * v.qq[...].astype(F32))).astype(BF16)

    for t in (t_ids, t_q, t_qq, t_pp, t_p, t_r, t_x, t_pos, t_sums, t_e, *t_y, t_totl, t_toth, t_inv, t_pw, *t_z, t_g):
        t.wait_send()
    forward(0).wait_send()
    forward(1).wait_send()
    send_n.wait_send()


def settle_kernel(q, p, n, oq, op, on):
    oq[...] = q[...]
    op[...] = p[...]
    on[...] = n[...]


def shards(query_hidden, passage_hidden, pool_hidden, query_proj, passage_proj, negative_ids):
    scratch = [pltpu.VMEM(shape, dtype) for shape, dtype in SCRATCH.values()]
    for n in PAIRS.values():
        scratch += [pltpu.SemaphoreType.DMA((n,)), pltpu.SemaphoreType.DMA((n,))]
    scratch.append(pltpu.SemaphoreType.DMA((16,)))
    results = pl.pallas_call(
        step_kernel,
        out_shape=[jax.ShapeDtypeStruct((n, EMB), BF16) for n in (QB, QB, 512)],
        in_specs=[pl.BlockSpec(memory_space=pl.ANY)] * 6,
        out_specs=[pl.BlockSpec(memory_space=pltpu.VMEM)] * 3,
        scratch_shapes=scratch,
        compiler_params=pltpu.CompilerParams(
            collective_id=1, has_side_effects=True, vmem_limit_bytes=60 * 1024 * 1024
        ),
        name="contrastive_step",
    )(query_proj, passage_proj, query_hidden, passage_hidden, pool_hidden, negative_ids.T)
    return pl.pallas_call(
        settle_kernel,
        out_shape=[jax.ShapeDtypeStruct((n, EMB), BF16) for n in (QB, QB, 512)],
        in_specs=[pl.BlockSpec(memory_space=pltpu.VMEM)] * 3,
        out_specs=[pl.BlockSpec(memory_space=pltpu.VMEM)] * 3,
        name="settle",
    )(*results)


def solution(mesh):
    placed = (
        P("dp", None),
        P(("tower", "dp"), None),
        P(("tower", "dp"), None),
        P(),
        P(),
        P("dp", None),
    )
    return jax.shard_map(
        shards,
        mesh=mesh,
        in_specs=placed,
        out_specs=(P(("dp", "tower"), None), P(("tower", "dp"), None), P(("tower", "dp"), None)),
        check_vma=False,
    )
```

```python
import jax
import jax.numpy as jnp
from jax import lax
from jax.experimental import pallas as pl
from jax.experimental.pallas import tpu as pltpu
from jax.sharding import PartitionSpec as P

logit_scale = 50.0
MESH = pl.DeviceIdType.MESH
F32 = jnp.float32
BF16 = jnp.bfloat16
I32 = jnp.int32
EMB = 768
CAP = 12
SLOTS = 2 * CAP
QB = 48
QD = 192
NN = (((1,), (0,)), ((), ()))
NT = (((1,), (1,)), ((), ()))
TN = (((0,), (0,)), ((), ()))


def mm(a, b, dims=NN):
    return lax.dot_general(a, b, dims, preferred_element_type=F32)


def rem(a, n):
    return lax.rem(a, n)


def quo(a, n):
    return lax.div(a, n)


def loop(lo, hi, body):
    def step(i, carry):
        body(i)
        return carry

    lax.fori_loop(lo, hi, step, 0)


def place():
    y = lax.axis_index("tower")
    dp = lax.axis_index("dp")
    return y, dp, quo(dp, 8), rem(quo(dp, 2), 4), rem(dp, 2)


class Route:
    def __init__(self, count, dest, source, slot, own, item=None):
        self.count, self.dest, self.source = count, dest, source
        self.slot, self.own, self.item = slot, own, item


def make_routes():
    y, dp, z, x, c = place()
    line = x * 2 + c
    turn = rem(y + 8 - z, 4)
    lead = quo(z, 4) * 4 + y
    at_home = rem(2 * z, 4) == y

    def plane_core(i):
        n = rem(x * 4 + y + i, 16)
        return rem(n, 4), z * 8 + quo(n, 4) * 2 + c

    def xline(i):
        return y, z * 8 + rem(x + i, 4) * 2 + c

    def yline(i):
        return rem(y + i, 4), dp

    def zcore(i):
        g = rem(z * 2 + c + i, 16)
        zz = quo(g, 2)
        return rem(turn + zz, 4), zz * 8 + x * 2 + rem(g, 2)

    def zline(i):
        zz = rem(z + i, 8)
        return rem(turn + zz, 4), zz * 8 + line

    def holder(i):
        zz = rem(z + i, 8)
        return rem(z + zz, 4), zz * 8 + line

    def column(i):
        return y, (turn + 4 * rem(quo(z, 4) + i, 2)) * 8 + line

    def home(i):
        k = rem(lead + i, 8)
        return rem(k, 4), (turn + 4 * quo(k, 4)) * 8 + line

    to_query = (rem(dp, 4), y * 16 + quo(dp, 4))
    to_passage = (quo(dp, 16), rem(dp, 16) * 4 + y)
    query_own = (to_query[0] == y) & (to_query[1] == dp)
    passage_own = (to_passage[0] == y) & (to_passage[1] == dp)
    return {
        "plane_core": Route(16, plane_core, plane_core, x * 4 + y, True),
        "xline": Route(4, xline, xline, x, True, lambda i: rem(x + i, 4)),
        "yline": Route(4, yline, yline, y, True, lambda i: rem(y + i, 4)),
        "zline": Route(8, zline, zline, z, True),
        "zcore": Route(16, zcore, zcore, z * 2 + c, True),
        "column": Route(2, column, column, quo(z, 4), at_home),
        "holder": Route(8, holder, home, lead, at_home),
        "home": Route(8, home, holder, z, at_home, lambda i: rem(lead + i, 8)),
        "to_query": Route(1, lambda i: to_query, lambda i: to_passage, 0, query_own),
        "to_passage": Route(1, lambda i: to_passage, lambda i: to_query, 0, passage_own),
    }


def each(route, far, near):
    if route.own is True:
        near()
    else:

        @pl.when(route.own)
        def _():
            near()

        @pl.when(jnp.logical_not(route.own))
        def _():
            far(0)

    if route.count > 1:
        loop(1, route.count, far)


class Transfer:
    def __init__(self, route, src, into, sems):
        self.route, self.src, self.into = route, src, into
        self.send_sem, self.recv_sem = sems[0].at[0], sems[1].at[0]

    def spot(self):
        return self.into if self.route.count == 1 else self.into.at[self.route.slot]

    def copy(self, i):
        return pltpu.make_async_remote_copy(
            src_ref=self.src(i),
            dst_ref=self.spot(),
            send_sem=self.send_sem,
            recv_sem=self.recv_sem,
            device_id=self.route.dest(i),
            device_id_type=MESH,
        )

    def local(self):
        return pltpu.make_async_copy(self.src(0), self.spot(), self.recv_sem)

    def start(self):
        each(self.route, lambda i: self.copy(i).start(), lambda: self.local().start())

    def wait_recv(self):
        pltpu.make_async_copy(self.into, self.into, self.recv_sem).wait()

    def wait_send(self):
        def taken(n):
            part = self.into if n == self.route.count else self.into.at[pl.ds(0, n)]
            pltpu.make_async_copy(part, part, self.send_sem).wait()

        n = self.route.count
        if self.route.own is True:
            taken(n - 1)
        else:
            if n > 1:

                @pl.when(self.route.own)
                def _():
                    taken(n - 1)

            @pl.when(jnp.logical_not(self.route.own))
            def _():
                taken(n)


class PlaneTransfer:
    def __init__(self, src, dst, sems, spots):
        self.src, self.dst, self.spots = src, dst, spots
        self.send_sem, self.recv_sem = sems[0].at[0], sems[1]
        y, dp, z, x, c = place()
        self.y, self.base, self.me = y, z * 8, y * 8 + x * 2 + c

    def start_row(self, row, first):
        def far(spot):
            pltpu.make_async_remote_copy(
                src_ref=self.src.at[row * 8 + spot],
                dst_ref=self.dst.at[self.me],
                send_sem=self.send_sem,
                recv_sem=self.recv_sem.at[self.y],
                device_id=(row, self.base + spot),
                device_id_type=MESH,
            ).start()

        def near():
            pltpu.make_async_copy(self.src.at[self.me], self.dst.at[self.me], self.recv_sem.at[self.y]).start()

        if isinstance(first, bool):
            near() if first else far(self.spots[0])
        else:
            pl.when(first)(near)
            pl.when(jnp.logical_not(first))(lambda: far(self.spots[0]))

        for spot in self.spots[1:]:
            far(spot)

    def wait_row(self, row):
        part = self.dst.at[pl.ds(row * 8, 8)]
        pltpu.make_async_copy(part, part, self.recv_sem.at[row]).wait()

    def wait_send(self):
        part = self.src.at[pl.ds(0, 31)]
        pltpu.make_async_copy(part, part, self.send_sem).wait()


def lane_of(shape):
    return lax.broadcasted_iota(I32, shape, len(shape) - 1)


def pack(column, base=0):
    groups = column.shape[0] // 8
    lane = lane_of((8, 128)) - base
    tile = jnp.zeros((8, 128), F32)
    for g in range(groups):
        tile = jnp.where(lane == g, column[8 * g : 8 * g + 8], tile)
    return tile


def unpack(tile, groups, base=0):
    lane = lane_of((8, 128)) - base
    parts = [jnp.sum(jnp.where(lane == g, tile, 0.0), axis=1, keepdims=True) for g in range(groups)]
    return jnp.concatenate(parts, axis=0)


def pack_slots(column):
    split = column.reshape(8, 3, 8, 1)
    lane = lane_of((8, 8, 128))
    tile = jnp.zeros((8, 8, 128), F32)
    for g in range(3):
        tile = jnp.where(lane == g, split[:, g], tile)
    return tile


def unpack_slots(tile):
    lane = lane_of((8, 8, 128))
    parts = [jnp.sum(jnp.where(lane == g, tile, 0.0), axis=2, keepdims=True)[:, None] for g in range(3)]
    return jnp.concatenate(parts, axis=1).reshape(QD, 1)


def three_parts(column):
    high = column.astype(BF16).astype(F32)
    rest = column - high
    middle = rest.astype(BF16).astype(F32)
    low = rest - middle
    lane = lane_of((column.shape[0], 128))
    parts = jnp.where(lane == 0, high, jnp.where(lane == 1, middle, jnp.where(lane == 2, low, 0.0)))
    return parts.astype(BF16)


def unit(projected):
    length = jnp.sqrt(jnp.sum(projected * projected, axis=1, keepdims=True) + 1e-06)
    return (projected / length).astype(BF16)


def flat(block):
    return block.astype(F32).reshape(block.shape[0] * block.shape[1], EMB)


SCRATCH = dict(
    wq=((2304, EMB), BF16),
    wp=((3072, EMB), BF16),
    hq=((QD, 2304), BF16),
    hp=((QB, 3072), BF16),
    hpool=((512, 3072), BF16),
    q192=((QD, EMB), BF16),
    p48=((QB, EMB), BF16),
    pool=((512, EMB), BF16),
    ids=((8, QD), I32),
    idh=((2, 8, QD), I32),
    qh=((2, 2, QD, EMB), BF16),
    ph=((16, QB, EMB), BF16),
    pp=((QB, EMB), BF16),
    qq=((QB, EMB), BF16),
    pick=((2, 768, QD), BF16),
    xs=((32, SLOTS, EMB), BF16),
    xr=((32, SLOTS, EMB), BF16),
    rs=((32, 8, 128), F32),
    rr=((32, 8, 128), F32),
    e=((768, 768), BF16),
    sums=((8, 128), F32),
    sumr=((16, 8, 128), F32),
    pos=((8, 128), F32),
    posr=((8, 8, 128), F32),
    nq=((768, EMB), F32),
    ns=((384, EMB), BF16),
    nr=((384, EMB), BF16),
    qn=((768, EMB), BF16),
    gs=((768, EMB), BF16),
    gx=((4, QD, EMB), BF16),
    gy=((QD, EMB), BF16),
    gr=((4, QB, EMB), BF16),
    chosen=((768, 512), BF16),
    ys=((2, 32, SLOTS, EMB // 2), BF16),
    yr=((2, 32, SLOTS, EMB // 2), BF16),
    es=((32, 8, 128), F32),
    er=((32, 8, 128), F32),
    tot=((8, 128), F32),
    totl=((8, 8, 128), F32),
    toth=((8, 8, 128), F32),
    invs=((32, 8, 128), F32),
    invr=((32, 8, 128), F32),
    hard=((2, QD, EMB), F32),
    zs=((2, 8, QB, EMB // 2), BF16),
    zr=((2, 8, QB, EMB // 2), BF16),
    pws=((8, 128), F32),
    pwr=((8, 128), F32),
    xw=((768, EMB), BF16),
)
PAIRS = dict(
    ids=1, q=1, p=1, pp=1, qq=1, fwd=2, x=4, r=4, sums=1, pos=1, n=1, y=4, y1=4, e=4, totl=1, toth=1, inv=4, z=1, z1=1, gx=1, g=1, pw=1
)


class Bag:
    pass


def step_kernel(wq, wp, hq, hp, hpool, ids, oq, op, on, *refs):
    v = Bag()
    for name, ref in zip(SCRATCH, refs):
        setattr(v, name, ref)
    rest = refs[len(SCRATCH) :]
    s = {name: (rest[2 * i], rest[2 * i + 1]) for i, name in enumerate(PAIRS)}
    in_sem = rest[2 * len(PAIRS)]
    routes = make_routes()
    y, dp, z, x, c = place()
    line = x * 2 + c
    turn = rem(y + 8 - z, 4)
    lead = quo(z, 4) * 4 + y

    loads = {}
    at = 0
    for name, ref, into, pieces in (
        ("ids", ids, v.ids, 1),
        ("hq", hq, v.hq, 2),
        ("wq", wq, v.wq, 4),
        ("hp", hp, v.hp, 1),
        ("wp", wp, v.wp, 4),
        ("hpool", hpool, v.hpool, 4),
    ):
        size = into.shape[0] // pieces
        loads[name] = []
        for k in range(pieces):
            part = pl.ds(k * size, size)
            loads[name].append(pltpu.make_async_copy(ref.at[part], into.at[part], in_sem.at[at]))
            at += 1

    def fetch(*names):
        for name in names:
            for load in loads[name]:
                load.start()

    fetch("ids", "hq", "wq")

    def loaded(*names):
        for name in names:
            for load in loads[name]:
                load.wait()

    barrier = pltpu.get_barrier_semaphore()

    def greet(ty, td):
        pl.semaphore_signal(barrier, inc=1, device_id=(ty, td), device_id_type=MESH)

    wanted = 0
    for name in ("column", "holder", "home", "to_query", "to_passage", "zcore"):
        route = routes[name]
        each(route, lambda i, route=route: greet(*route.source(i)), lambda: None)
        wanted = wanted + route.count - 1
        if route.own is not True:
            wanted = wanted + jnp.where(route.own, 0, 1)

    def greet_plane(i):
        m = rem(y * 8 + line + i, 32)
        greet(quo(m, 8), z * 8 + rem(m, 8))

    loop(1, 32, greet_plane)
    wanted = wanted + 31

    fetch("hp", "wp")
    loaded("ids", "hq", "wq")
    fetch("hpool")
    v.q192[...] = unit(mm(v.hq[...], v.wq[...]))
    own_q = v.q192.at[pl.ds(pl.multiple_of(y * QB, QB), QB), :]
    pl.semaphore_wait(barrier, wanted)
    t_ids = Transfer(routes["column"], lambda i: v.ids, v.idh, s["ids"])
    t_q = Transfer(routes["column"], lambda i: v.q192, v.qh.at[c], s["q"])
    t_qq = Transfer(routes["to_passage"], lambda i: own_q, v.qq, s["qq"])
    t_ids.start()
    t_q.start()
    loaded("hp", "wp")
    v.p48[...] = unit(mm(v.hp[...], v.wp[...]))
    t_p = Transfer(routes["plane_core"], lambda i: v.p48, v.ph, s["p"])
    t_pp = Transfer(routes["to_query"], lambda i: v.p48, v.pp, s["pp"])
    t_p.start()
    loaded("hpool")

    def project_pool(i):
        part = pl.ds(pl.multiple_of(i * 256, 256), 256)
        v.pool[part, :] = unit(mm(v.hpool[part, :], v.wp[...]))

    loop(0, 2, project_pool)

    t_ids.wait_recv()
    before = (lax.broadcasted_iota(I32, (QD, QD), 0) < lane_of((QD, QD))).astype(F32).astype(BF16)
    member_row = lax.broadcasted_iota(I32, (32, QD), 0)
    slots, codes = [], []
    for half in range(2):
        held = v.idh[half]
        owner = lax.shift_right_logical(held, 9)
        inside = (lax.shift_right_logical(owner, 3) & 7) == z
        target = jnp.where(inside, lax.shift_right_logical(owner, 6) * 8 + (owner & 7), -1)
        code = ((held & 511) + 1).astype(F32)
        names = [(member_row == target[k : k + 1]).astype(F32) for k in range(8)]
        count = names[0]
        for k in range(1, 8):
            count = count + names[k]
        running = mm(count.astype(BF16), before)
        start = (target * SLOTS + half * CAP).astype(F32)
        rows = []
        for k in range(8):
            rank = jnp.sum(names[k] * running, axis=0, keepdims=True)
            rows.append(jnp.where(target[k : k + 1] >= 0, start[k : k + 1] + rank, -1.0))
            running = running + names[k]
        slots.append(rows)
        codes.append([code[k : k + 1] for k in range(8)])

    def forward(k):
        return pltpu.make_async_remote_copy(
            src_ref=v.qh.at[c, k],
            dst_ref=v.qh.at[c, k],
            send_sem=s["fwd"][0].at[k],
            recv_sem=s["fwd"][1].at[k],
            device_id=(y, dp + 1 - 2 * c),
            device_id_type=MESH,
        )

    t_q.wait_recv()
    forward(0).start()
    forward(1).start()

    spots = [rem(line + t, 8) for t in range(8)]
    t_x = PlaneTransfer(v.xs, v.xr, s["x"], spots)
    t_r = PlaneTransfer(v.rs, v.rr, s["r"], spots)

    def ask(j):
        row = rem(y + j, 4)
        here = pl.ds(pl.multiple_of(row * QD, QD), QD)
        spot = (lax.broadcasted_iota(I32, (QD, QD), 0) + row * QD).astype(F32)
        found = jnp.zeros((QD, QD), F32)
        asked = jnp.zeros((QD, EMB), F32)
        for half in range(2):
            hits = jnp.zeros((QD, QD), F32)
            for k in range(8):
                hits = jnp.where(spot == slots[half][k], codes[half][k], hits)
            found = found + hits
            picked = jnp.where(hits > 0.0, 1.0, 0.0).astype(BF16)
            v.pick[half, here, :] = picked
            asked = asked + mm(picked, v.qh[c, half])
        v.xs[pl.ds(row * 8, 8)] = asked.reshape(8, SLOTS, EMB).astype(BF16)
        v.rs[pl.ds(row * 8, 8)] = pack_slots(jnp.sum(found, axis=1, keepdims=True))
        t_r.start_row(row, j == 0)
        t_x.start_row(row, j == 0)

    loop(0, 4, ask)

    t_pp.start()

    t_p.wait_recv()

    def taken(k):
        pltpu.make_async_copy(v.qh.at[1 - c, k], v.qh.at[1 - c, k], s["fwd"][1].at[k]).wait()

    taken(0)
    taken(1)

    def queries(j):
        return v.qh[quo(j, 2), rem(j, 2)]

    def score(j, tile):
        here = pl.ds(pl.multiple_of(j * QD, QD), QD)
        passages = v.ph[...].reshape(768, EMB)
        grown = jnp.exp(logit_scale * mm(queries(j), passages, NT))
        low = grown.astype(BF16)
        v.e[here, :] = low
        v.nq[here, :] = mm(low, passages)
        return tile + pack(jnp.sum(grown, axis=1, keepdims=True), j * 24)

    v.sums[...] = lax.fori_loop(0, 4, score, jnp.zeros((8, 128), F32))
    t_sums = Transfer(routes["zcore"], lambda i: v.sums, v.sumr, s["sums"])
    t_sums.start()
    v.ns[...] = v.nq[pl.ds(pl.multiple_of((1 - c) * 384, 384), 384), :].astype(BF16)
    send_n = pltpu.make_async_remote_copy(
        src_ref=v.ns,
        dst_ref=v.nr,
        send_sem=s["n"][0].at[0],
        recv_sem=s["n"][1].at[0],
        device_id=(y, dp + 1 - 2 * c),
        device_id_type=MESH,
    )
    send_n.start()
    t_sums.wait_recv()
    inv_batch = 1.0 / jnp.where(lane_of((8, 128)) < 96, jnp.sum(v.sumr[...], axis=0), 1.0)

    def scale_queries(j):
        here = pl.ds(pl.multiple_of(j * QD, QD), QD)
        v.qn[here, :] = (queries(j).astype(F32) * unpack(inv_batch, 24, j * 24)).astype(BF16)

    loop(0, 4, scale_queries)
    for j in range(3):
        v.gs[256 * j : 256 * j + 256, :] = mm(v.e[:, 256 * j : 256 * j + 256], v.qn[...], TN).astype(BF16)

    t_y = [PlaneTransfer(v.ys.at[h], v.yr.at[h], s[name], spots) for h, name in enumerate(("y", "y1"))]
    t_e = PlaneTransfer(v.es, v.er, s["e"], spots)

    def answer(j):
        row = rem(y + 4 - j, 4)
        here = pl.ds(pl.multiple_of(row * QD, QD), QD)
        t_r.wait_row(row)
        t_x.wait_row(row)
        code = unpack_slots(v.rr[pl.ds(row * 8, 8)])
        chosen = jnp.where(code == (lane_of((QD, 512)) + 1).astype(F32), 1.0, 0.0).astype(BF16)
        v.chosen[here, :] = chosen
        named = mm(chosen, v.pool[...])
        asked = flat(v.xr[pl.ds(row * 8, 8)])
        neg_exp = jnp.exp(logit_scale * jnp.sum(asked * named, axis=1, keepdims=True))
        v.es[pl.ds(row * 8, 8)] = pack_slots(neg_exp)
        t_e.start_row(row, j == 0)
        rows = (neg_exp * named).reshape(8, SLOTS, EMB).astype(BF16)
        for h in range(2):
            v.ys[h, pl.ds(row * 8, 8)] = rows[:, :, 384 * h : 384 * h + 384]

    loop(0, 4, answer)
    t_qq.start()

    def give(h, j):
        t_y[h].start_row(rem(y + 4 - j, 4), j == 0)

    give(0, 0)

    t_pp.wait_recv()
    pos_exp = jnp.exp(logit_scale * jnp.sum(own_q[...].astype(F32) * v.pp[...].astype(F32), axis=1, keepdims=True))
    v.pos[...] = pack(pos_exp, lead * 6)
    t_pos = Transfer(routes["holder"], lambda i: v.pos, v.posr, s["pos"])
    t_pos.start()

    def total(j, carry):
        row = rem(y + j, 4)
        here = pl.ds(pl.multiple_of(row * QD, QD), QD)
        t_e.wait_row(row)
        parts = three_parts(unpack_slots(v.er[pl.ds(row * 8, 8)]))
        return tuple(carry[half] + mm(v.pick[half, here, :], parts, TN) for half in range(2))

    both = lax.fori_loop(0, 4, total, (jnp.zeros((QD, 128), F32), jnp.zeros((QD, 128), F32)))
    column = jnp.concatenate([jnp.sum(t, axis=1, keepdims=True) for t in both], axis=0)
    v.tot[...] = pack(column)
    t_totl = Transfer(routes["zline"], lambda i: v.tot, v.totl, s["totl"])
    t_toth = Transfer(routes["home"], lambda i: v.tot, v.toth, s["toth"])
    t_totl.start()
    t_toth.start()
    loop(1, 4, lambda j: give(0, j))
    loop(0, 4, lambda j: give(1, j))

    across = routes["xline"]
    t_gx = Transfer(
        across,
        lambda i: v.gs.at[pl.ds(pl.multiple_of(across.item(i) * QD, QD), QD), :],
        v.gx,
        s["gx"],
    )
    t_gx.start()

    t_pos.wait_recv()
    t_totl.wait_recv()
    hard_total = jnp.sum(v.totl[...], axis=0) + jnp.sum(v.posr[...], axis=0)
    inv_hard_tile = 1.0 / jnp.where(lane_of((8, 128)) < 48, hard_total, 1.0)
    inv_hard = [unpack(inv_hard_tile, 24, 24 * half) for half in range(2)]
    inv_parts = [three_parts(inv_hard[half]) for half in range(2)]
    t_inv = PlaneTransfer(v.invs, v.invr, s["inv"], spots)

    def tell(j):
        row = rem(y + j, 4)
        here = pl.ds(pl.multiple_of(row * QD, QD), QD)
        shares = mm(v.pick[0, here, :], inv_parts[0]) + mm(v.pick[1, here, :], inv_parts[1])
        v.invs[pl.ds(row * 8, 8)] = pack_slots(jnp.sum(shares, axis=1, keepdims=True))
        t_inv.start_row(row, j == 0)

    loop(0, 4, tell)
    t_toth.wait_recv()
    own_total = unpack(jnp.sum(v.toth[...], axis=0), 6, lead * 6)
    pos_coef = pos_exp / (pos_exp + own_total) - 2.0
    v.pws[...] = pack(pos_coef)
    t_pw = Transfer(routes["to_passage"], lambda i: v.pws, v.pwr, s["pw"])
    t_pw.start()

    v.hard[...] = jnp.zeros((2, QD, EMB), F32)

    def collect(h):
        lanes = slice(384 * h, 384 * h + 384)

        def gather(j):
            row = rem(y + j, 4)
            here = pl.ds(pl.multiple_of(row * QD, QD), QD)
            t_y[h].wait_row(row)
            rows = v.yr[h, pl.ds(row * 8, 8)].astype(F32).reshape(QD, 384).astype(BF16)
            for half in range(2):
                v.hard[half, :, lanes] += mm(v.pick[half, here, :], rows, TN)

        loop(0, 4, gather)
        for half in range(2):
            own = v.nq[pl.ds(pl.multiple_of(c * 384 + half * QD, QD), QD), lanes]
            mine = own + v.nr[half * QD : half * QD + QD, lanes].astype(F32)
            inv_own = unpack(inv_batch, 24, c * 48 + half * 24)
            mixed = mine * inv_own + v.hard[half, :, lanes] * inv_hard[half]
            v.zs[h, 4 * half : 4 * half + 4] = mixed.astype(BF16).reshape(4, QB, 384)

    home = routes["home"]
    t_z = [
        Transfer(home, lambda i, h=h: v.zs.at[h, home.item(i)], v.zr.at[h], s[name])
        for h, name in enumerate(("z", "z1"))
    ]
    pltpu.make_async_copy(v.nr, v.nr, s["n"][1].at[0]).wait()
    collect(0)
    t_z[0].start()
    collect(1)
    t_z[1].start()

    t_gx.wait_recv()
    v.gy[...] = jnp.sum(v.gx[...].astype(F32), axis=0).astype(BF16)
    along = routes["yline"]
    t_g = Transfer(
        along, lambda i: v.gy.at[pl.ds(pl.multiple_of(along.item(i) * QB, QB), QB), :], v.gr, s["g"]
    )
    t_g.start()

    def weigh(j):
        row = rem(y + 4 - j, 4)
        here = pl.ds(pl.multiple_of(row * QD, QD), QD)
        t_inv.wait_row(row)
        share = unpack_slots(v.es[pl.ds(row * 8, 8)]) * unpack_slots(v.invr[pl.ds(row * 8, 8)])
        v.xw[here, :] = (flat(v.xr[pl.ds(row * 8, 8)]) * share).astype(BF16)

    loop(0, 4, weigh)
    for j in range(2):
        part = mm(v.chosen[:, 256 * j : 256 * j + 256], v.xw[...], TN)
        on[256 * j : 256 * j + 256, :] = (logit_scale * part).astype(BF16)

    for h in range(2):
        t_z[h].wait_recv()
        lanes = slice(384 * h, 384 * h + 384)
        summed = jnp.sum(v.zr[h].astype(F32), axis=0)
        oq[:, lanes] = (logit_scale * (summed + pos_coef * v.pp[:, lanes].astype(F32))).astype(BF16)
    t_pw.wait_recv()
    t_qq.wait_recv()
    t_g.wait_recv()
    summed = jnp.sum(v.gr[...].astype(F32), axis=0)
    coef = unpack(v.pwr[...], 6)
    op[...] = (logit_scale * (summed + coef * v.qq[...].astype(F32))).astype(BF16)

    for t in (t_ids, t_q, t_qq, t_pp, t_p, t_r, t_x, t_pos, t_sums, t_e, *t_y, t_totl, t_toth, t_inv, t_pw, *t_z, t_gx, t_g):
        t.wait_send()
    forward(0).wait_send()
    forward(1).wait_send()
    send_n.wait_send()


def settle_kernel(q, p, n, oq, op, on):
    oq[...] = q[...]
    op[...] = p[...]
    on[...] = n[...]


def shards(query_hidden, passage_hidden, pool_hidden, query_proj, passage_proj, negative_ids):
    scratch = [pltpu.VMEM(shape, dtype) for shape, dtype in SCRATCH.values()]
    for n in PAIRS.values():
        scratch += [pltpu.SemaphoreType.DMA((n,)), pltpu.SemaphoreType.DMA((n,))]
    scratch.append(pltpu.SemaphoreType.DMA((16,)))
    results = pl.pallas_call(
        step_kernel,
        out_shape=[jax.ShapeDtypeStruct((n, EMB), BF16) for n in (QB, QB, 512)],
        in_specs=[pl.BlockSpec(memory_space=pl.ANY)] * 6,
        out_specs=[pl.BlockSpec(memory_space=pltpu.VMEM)] * 3,
        scratch_shapes=scratch,
        compiler_params=pltpu.CompilerParams(
            collective_id=1, has_side_effects=True, vmem_limit_bytes=60 * 1024 * 1024
        ),
        name="contrastive_step",
    )(query_proj, passage_proj, query_hidden, passage_hidden, pool_hidden, negative_ids.T)
    return pl.pallas_call(
        settle_kernel,
        out_shape=[jax.ShapeDtypeStruct((n, EMB), BF16) for n in (QB, QB, 512)],
        in_specs=[pl.BlockSpec(memory_space=pltpu.VMEM)] * 3,
        out_specs=[pl.BlockSpec(memory_space=pltpu.VMEM)] * 3,
        name="settle",
    )(*results)


def solution(mesh):
    placed = (
        P("dp", None),
        P(("tower", "dp"), None),
        P(("tower", "dp"), None),
        P(),
        P(),
        P("dp", None),
    )
    return jax.shard_map(
        shards,
        mesh=mesh,
        in_specs=placed,
        out_specs=(P(("dp", "tower"), None), P(("tower", "dp"), None), P(("tower", "dp"), None)),
        check_vma=False,
    )
```

```python
import jax
import jax.numpy as jnp
from jax import lax
from jax.experimental import pallas as pl
from jax.experimental.pallas import tpu as pltpu
from jax.sharding import PartitionSpec as P

logit_scale = 50.0
MESH = pl.DeviceIdType.MESH
F32 = jnp.float32
BF16 = jnp.bfloat16
I32 = jnp.int32
EMB = 768
CAP = 12
SLOTS = 2 * CAP
QB = 48
QD = 192
NN = (((1,), (0,)), ((), ()))
NT = (((1,), (1,)), ((), ()))
TN = (((0,), (0,)), ((), ()))


def mm(a, b, dims=NN):
    return lax.dot_general(a, b, dims, preferred_element_type=F32)


def rem(a, n):
    return lax.rem(a, n)


def quo(a, n):
    return lax.div(a, n)


def loop(lo, hi, body):
    def step(i, carry):
        body(i)
        return carry

    lax.fori_loop(lo, hi, step, 0)


def place():
    y = lax.axis_index("tower")
    dp = lax.axis_index("dp")
    return y, dp, quo(dp, 8), rem(quo(dp, 2), 4), rem(dp, 2)


class Route:
    def __init__(self, count, dest, source, slot, own, item=None):
        self.count, self.dest, self.source = count, dest, source
        self.slot, self.own, self.item = slot, own, item


def make_routes():
    y, dp, z, x, c = place()
    line = x * 2 + c
    turn = rem(y + 8 - z, 4)
    lead = quo(z, 4) * 4 + y
    at_home = rem(2 * z, 4) == y

    def plane_core(i):
        n = rem(x * 4 + y + i, 16)
        return rem(n, 4), z * 8 + quo(n, 4) * 2 + c

    def xline(i):
        return y, z * 8 + rem(x + i, 4) * 2 + c

    def yline(i):
        return rem(y + i, 4), dp

    def zcore(i):
        g = rem(z * 2 + c + i, 16)
        zz = quo(g, 2)
        return rem(turn + zz, 4), zz * 8 + x * 2 + rem(g, 2)

    def zline(i):
        zz = rem(z + i, 8)
        return rem(turn + zz, 4), zz * 8 + line

    def holder(i):
        zz = rem(z + i, 8)
        return rem(z + zz, 4), zz * 8 + line

    def column(i):
        return y, (turn + 4 * rem(quo(z, 4) + i, 2)) * 8 + line

    def home(i):
        k = rem(lead + i, 8)
        return rem(k, 4), (turn + 4 * quo(k, 4)) * 8 + line

    to_query = (rem(dp, 4), y * 16 + quo(dp, 4))
    to_passage = (quo(dp, 16), rem(dp, 16) * 4 + y)
    query_own = (to_query[0] == y) & (to_query[1] == dp)
    passage_own = (to_passage[0] == y) & (to_passage[1] == dp)
    return {
        "plane_core": Route(16, plane_core, plane_core, x * 4 + y, True),
        "xline": Route(4, xline, xline, x, True, lambda i: rem(x + i, 4)),
        "yline": Route(4, yline, yline, y, True, lambda i: rem(y + i, 4)),
        "zline": Route(8, zline, zline, z, True),
        "zcore": Route(16, zcore, zcore, z * 2 + c, True),
        "column": Route(2, column, column, quo(z, 4), at_home),
        "holder": Route(8, holder, home, lead, at_home),
        "home": Route(8, home, holder, z, at_home, lambda i: rem(lead + i, 8)),
        "to_query": Route(1, lambda i: to_query, lambda i: to_passage, 0, query_own),
        "to_passage": Route(1, lambda i: to_passage, lambda i: to_query, 0, passage_own),
    }


def each(route, far, near):
    if route.own is True:
        near()
    else:

        @pl.when(route.own)
        def _():
            near()

        @pl.when(jnp.logical_not(route.own))
        def _():
            far(0)

    if route.count > 1:
        loop(1, route.count, far)


class Transfer:
    def __init__(self, route, src, into, sems):
        self.route, self.src, self.into = route, src, into
        self.send_sem, self.recv_sem = sems[0].at[0], sems[1].at[0]

    def spot(self):
        return self.into if self.route.count == 1 else self.into.at[self.route.slot]

    def copy(self, i):
        return pltpu.make_async_remote_copy(
            src_ref=self.src(i),
            dst_ref=self.spot(),
            send_sem=self.send_sem,
            recv_sem=self.recv_sem,
            device_id=self.route.dest(i),
            device_id_type=MESH,
        )

    def local(self):
        return pltpu.make_async_copy(self.src(0), self.spot(), self.recv_sem)

    def start(self):
        each(self.route, lambda i: self.copy(i).start(), lambda: self.local().start())

    def wait_recv(self):
        pltpu.make_async_copy(self.into, self.into, self.recv_sem).wait()

    def wait_send(self):
        def taken(n):
            part = self.into if n == self.route.count else self.into.at[pl.ds(0, n)]
            pltpu.make_async_copy(part, part, self.send_sem).wait()

        n = self.route.count
        if self.route.own is True:
            taken(n - 1)
        else:
            if n > 1:

                @pl.when(self.route.own)
                def _():
                    taken(n - 1)

            @pl.when(jnp.logical_not(self.route.own))
            def _():
                taken(n)


class PlaneTransfer:
    def __init__(self, src, dst, sems, spots):
        self.src, self.dst, self.spots = src, dst, spots
        self.send_sem, self.recv_sem = sems[0].at[0], sems[1]
        y, dp, z, x, c = place()
        self.y, self.base, self.me = y, z * 8, y * 8 + x * 2 + c

    def start_row(self, row, first):
        def far(spot):
            pltpu.make_async_remote_copy(
                src_ref=self.src.at[row * 8 + spot],
                dst_ref=self.dst.at[self.me],
                send_sem=self.send_sem,
                recv_sem=self.recv_sem.at[self.y],
                device_id=(row, self.base + spot),
                device_id_type=MESH,
            ).start()

        def near():
            pltpu.make_async_copy(self.src.at[self.me], self.dst.at[self.me], self.recv_sem.at[self.y]).start()

        if isinstance(first, bool):
            near() if first else far(self.spots[0])
        else:
            pl.when(first)(near)
            pl.when(jnp.logical_not(first))(lambda: far(self.spots[0]))

        for spot in self.spots[1:]:
            far(spot)

    def wait_row(self, row):
        part = self.dst.at[pl.ds(row * 8, 8)]
        pltpu.make_async_copy(part, part, self.recv_sem.at[row]).wait()

    def wait_send(self):
        part = self.src.at[pl.ds(0, 31)]
        pltpu.make_async_copy(part, part, self.send_sem).wait()


def lane_of(shape):
    return lax.broadcasted_iota(I32, shape, len(shape) - 1)


def pack(column, base=0):
    groups = column.shape[0] // 8
    lane = lane_of((8, 128)) - base
    tile = jnp.zeros((8, 128), F32)
    for g in range(groups):
        tile = jnp.where(lane == g, column[8 * g : 8 * g + 8], tile)
    return tile


def unpack(tile, groups, base=0):
    lane = lane_of((8, 128)) - base
    parts = [jnp.sum(jnp.where(lane == g, tile, 0.0), axis=1, keepdims=True) for g in range(groups)]
    return jnp.concatenate(parts, axis=0)


def pack_slots(column):
    split = column.reshape(8, 3, 8, 1)
    lane = lane_of((8, 8, 128))
    tile = jnp.zeros((8, 8, 128), F32)
    for g in range(3):
        tile = jnp.where(lane == g, split[:, g], tile)
    return tile


def unpack_slots(tile):
    lane = lane_of((8, 8, 128))
    parts = [jnp.sum(jnp.where(lane == g, tile, 0.0), axis=2, keepdims=True)[:, None] for g in range(3)]
    return jnp.concatenate(parts, axis=1).reshape(QD, 1)


def three_parts(column):
    high = column.astype(BF16).astype(F32)
    rest = column - high
    middle = rest.astype(BF16).astype(F32)
    low = rest - middle
    lane = lane_of((column.shape[0], 128))
    parts = jnp.where(lane == 0, high, jnp.where(lane == 1, middle, jnp.where(lane == 2, low, 0.0)))
    return parts.astype(BF16)


def unit(projected):
    length = jnp.sqrt(jnp.sum(projected * projected, axis=1, keepdims=True) + 1e-06)
    return (projected / length).astype(BF16)


def flat(block):
    return block.astype(F32).reshape(block.shape[0] * block.shape[1], EMB)


SCRATCH = dict(
    wq=((2304, EMB), BF16),
    wp=((3072, EMB), BF16),
    hq=((QD, 2304), BF16),
    hp=((QB, 3072), BF16),
    hpool=((512, 3072), BF16),
    q192=((QD, EMB), BF16),
    p48=((QB, EMB), BF16),
    pool=((512, EMB), BF16),
    ids=((8, QD), I32),
    idh=((2, 8, QD), I32),
    qh=((2, 2, QD, EMB), BF16),
    ph=((16, QB, EMB), BF16),
    pp=((QB, EMB), BF16),
    qq=((QB, EMB), BF16),
    pick=((2, 768, QD), BF16),
    xs=((32, SLOTS, EMB), BF16),
    xr=((32, SLOTS, EMB), BF16),
    rs=((32, 8, 128), F32),
    rr=((32, 8, 128), F32),
    e=((768, 768), BF16),
    sums=((8, 128), F32),
    sumr=((16, 8, 128), F32),
    pos=((8, 128), F32),
    posr=((8, 8, 128), F32),
    nq=((768, EMB), F32),
    ns=((384, EMB), BF16),
    nr=((384, EMB), BF16),
    qn=((768, EMB), BF16),
    gs=((768, EMB), BF16),
    gx=((4, QD, EMB), BF16),
    gy=((QD, EMB), BF16),
    gr=((4, QB, EMB), BF16),
    chosen=((768, 512), BF16),
    ys=((2, 32, SLOTS, EMB // 2), BF16),
    yr=((2, 32, SLOTS, EMB // 2), BF16),
    es=((32, 8, 128), F32),
    er=((32, 8, 128), F32),
    tot=((8, 128), F32),
    totl=((8, 8, 128), F32),
    toth=((8, 8, 128), F32),
    invs=((32, 8, 128), F32),
    invr=((32, 8, 128), F32),
    hard=((2, QD, EMB), F32),
    zs=((2, 8, QB, EMB // 2), BF16),
    zr=((2, 8, QB, EMB // 2), BF16),
    pws=((8, 128), F32),
    pwr=((8, 128), F32),
    xw=((768, EMB), BF16),
)
PAIRS = dict(
    ids=1, q=1, p=1, pp=1, qq=1, fwd=2, x=4, r=4, sums=1, pos=1, n=1, y=4, y1=4, e=4, totl=1, toth=1, inv=4, z=1, z1=1, gx=1, g=1, pw=1
)


class Bag:
    pass


def step_kernel(wq, wp, hq, hp, hpool, ids, oq, op, on, *refs):
    v = Bag()
    for name, ref in zip(SCRATCH, refs):
        setattr(v, name, ref)
    rest = refs[len(SCRATCH) :]
    s = {name: (rest[2 * i], rest[2 * i + 1]) for i, name in enumerate(PAIRS)}
    in_sem = rest[2 * len(PAIRS)]
    routes = make_routes()
    y, dp, z, x, c = place()
    line = x * 2 + c
    turn = rem(y + 8 - z, 4)
    lead = quo(z, 4) * 4 + y

    loads = {}
    at = 0
    for name, ref, into, pieces in (
        ("ids", ids, v.ids, 1),
        ("hq", hq, v.hq, 2),
        ("wq", wq, v.wq, 4),
        ("hp", hp, v.hp, 1),
        ("wp", wp, v.wp, 4),
        ("hpool", hpool, v.hpool, 4),
    ):
        size = into.shape[0] // pieces
        loads[name] = []
        for k in range(pieces):
            part = pl.ds(k * size, size)
            loads[name].append(pltpu.make_async_copy(ref.at[part], into.at[part], in_sem.at[at]))
            at += 1

    def fetch(*names):
        for name in names:
            for load in loads[name]:
                load.start()

    fetch("ids", "hq", "wq")

    def loaded(*names):
        for name in names:
            for load in loads[name]:
                load.wait()

    barrier = pltpu.get_barrier_semaphore()

    def greet(ty, td):
        pl.semaphore_signal(barrier, inc=1, device_id=(ty, td), device_id_type=MESH)

    wanted = 0
    for name in ("column", "holder", "home", "to_query", "to_passage", "zcore"):
        route = routes[name]
        each(route, lambda i, route=route: greet(*route.source(i)), lambda: None)
        wanted = wanted + route.count - 1
        if route.own is not True:
            wanted = wanted + jnp.where(route.own, 0, 1)

    def greet_plane(i):
        m = rem(y * 8 + line + i, 32)
        greet(quo(m, 8), z * 8 + rem(m, 8))

    loop(1, 32, greet_plane)
    wanted = wanted + 31

    fetch("hp", "wp")
    loaded("ids", "hq", "wq")
    fetch("hpool")
    v.q192[...] = unit(mm(v.hq[...], v.wq[...]))
    own_q = v.q192.at[pl.ds(pl.multiple_of(y * QB, QB), QB), :]
    pl.semaphore_wait(barrier, wanted)
    t_ids = Transfer(routes["column"], lambda i: v.ids, v.idh, s["ids"])
    t_q = Transfer(routes["column"], lambda i: v.q192, v.qh.at[c], s["q"])
    t_qq = Transfer(routes["to_passage"], lambda i: own_q, v.qq, s["qq"])
    t_ids.start()
    t_q.start()
    loaded("hp", "wp")
    v.p48[...] = unit(mm(v.hp[...], v.wp[...]))
    t_p = Transfer(routes["plane_core"], lambda i: v.p48, v.ph, s["p"])
    t_pp = Transfer(routes["to_query"], lambda i: v.p48, v.pp, s["pp"])
    t_p.start()
    loaded("hpool")

    def project_pool(i):
        part = pl.ds(pl.multiple_of(i * 256, 256), 256)
        v.pool[part, :] = unit(mm(v.hpool[part, :], v.wp[...]))

    loop(0, 2, project_pool)

    t_ids.wait_recv()
    before = (lax.broadcasted_iota(I32, (QD, QD), 0) < lane_of((QD, QD))).astype(F32).astype(BF16)
    member_row = lax.broadcasted_iota(I32, (32, QD), 0)
    slots, codes = [], []
    for half in range(2):
        held = v.idh[half]
        owner = lax.shift_right_logical(held, 9)
        inside = (lax.shift_right_logical(owner, 3) & 7) == z
        target = jnp.where(inside, lax.shift_right_logical(owner, 6) * 8 + (owner & 7), -1)
        code = ((held & 511) + 1).astype(F32)
        names = [(member_row == target[k : k + 1]).astype(F32) for k in range(8)]
        count = names[0]
        for k in range(1, 8):
            count = count + names[k]
        running = mm(count.astype(BF16), before)
        start = (target * SLOTS + half * CAP).astype(F32)
        rows = []
        for k in range(8):
            rank = jnp.sum(names[k] * running, axis=0, keepdims=True)
            rows.append(jnp.where(target[k : k + 1] >= 0, start[k : k + 1] + rank, -1.0))
            running = running + names[k]
        slots.append(rows)
        codes.append([code[k : k + 1] for k in range(8)])

    def forward(k):
        return pltpu.make_async_remote_copy(
            src_ref=v.qh.at[c, k],
            dst_ref=v.qh.at[c, k],
            send_sem=s["fwd"][0].at[k],
            recv_sem=s["fwd"][1].at[k],
            device_id=(y, dp + 1 - 2 * c),
            device_id_type=MESH,
        )

    t_q.wait_recv()
    forward(0).start()
    forward(1).start()

    spots = [rem(line + t, 8) for t in range(8)]
    t_x = PlaneTransfer(v.xs, v.xr, s["x"], spots)
    t_r = PlaneTransfer(v.rs, v.rr, s["r"], spots)

    def ask(j):
        row = rem(y + j, 4)
        here = pl.ds(pl.multiple_of(row * QD, QD), QD)
        spot = (lax.broadcasted_iota(I32, (QD, QD), 0) + row * QD).astype(F32)
        found = jnp.zeros((QD, QD), F32)
        asked = jnp.zeros((QD, EMB), F32)
        for half in range(2):
            hits = jnp.zeros((QD, QD), F32)
            for k in range(8):
                hits = jnp.where(spot == slots[half][k], codes[half][k], hits)
            found = found + hits
            picked = jnp.where(hits > 0.0, 1.0, 0.0).astype(BF16)
            v.pick[half, here, :] = picked
            asked = asked + mm(picked, v.qh[c, half])
        v.xs[pl.ds(row * 8, 8)] = asked.reshape(8, SLOTS, EMB).astype(BF16)
        v.rs[pl.ds(row * 8, 8)] = pack_slots(jnp.sum(found, axis=1, keepdims=True))
        t_r.start_row(row, j == 0)
        t_x.start_row(row, j == 0)

    loop(0, 4, ask)

    t_pp.start()

    t_p.wait_recv()

    def taken(k):
        pltpu.make_async_copy(v.qh.at[1 - c, k], v.qh.at[1 - c, k], s["fwd"][1].at[k]).wait()

    taken(0)
    taken(1)

    def queries(j):
        return v.qh[quo(j, 2), rem(j, 2)]

    def score(j, tile):
        here = pl.ds(pl.multiple_of(j * QD, QD), QD)
        passages = v.ph[...].reshape(768, EMB)
        grown = jnp.exp(logit_scale * mm(queries(j), passages, NT))
        low = grown.astype(BF16)
        v.e[here, :] = low
        v.nq[here, :] = mm(low, passages)
        return tile + pack(jnp.sum(grown, axis=1, keepdims=True), j * 24)

    v.sums[...] = lax.fori_loop(0, 4, score, jnp.zeros((8, 128), F32))
    t_sums = Transfer(routes["zcore"], lambda i: v.sums, v.sumr, s["sums"])
    t_sums.start()
    v.ns[...] = v.nq[pl.ds(pl.multiple_of((1 - c) * 384, 384), 384), :].astype(BF16)
    send_n = pltpu.make_async_remote_copy(
        src_ref=v.ns,
        dst_ref=v.nr,
        send_sem=s["n"][0].at[0],
        recv_sem=s["n"][1].at[0],
        device_id=(y, dp + 1 - 2 * c),
        device_id_type=MESH,
    )
    send_n.start()
    t_sums.wait_recv()
    inv_batch = 1.0 / jnp.where(lane_of((8, 128)) < 96, jnp.sum(v.sumr[...], axis=0), 1.0)

    def scale_queries(j):
        here = pl.ds(pl.multiple_of(j * QD, QD), QD)
        v.qn[here, :] = (queries(j).astype(F32) * unpack(inv_batch, 24, j * 24)).astype(BF16)

    loop(0, 4, scale_queries)
    for j in range(3):
        v.gs[256 * j : 256 * j + 256, :] = mm(v.e[:, 256 * j : 256 * j + 256], v.qn[...], TN).astype(BF16)

    t_y = [PlaneTransfer(v.ys.at[h], v.yr.at[h], s[name], spots) for h, name in enumerate(("y", "y1"))]
    t_e = PlaneTransfer(v.es, v.er, s["e"], spots)

    def answer(j):
        row = rem(y + 4 - j, 4)
        here = pl.ds(pl.multiple_of(row * QD, QD), QD)
        t_r.wait_row(row)
        t_x.wait_row(row)
        code = unpack_slots(v.rr[pl.ds(row * 8, 8)])
        chosen = jnp.where(code == (lane_of((QD, 512)) + 1).astype(F32), 1.0, 0.0).astype(BF16)
        v.chosen[here, :] = chosen
        named = mm(chosen, v.pool[...])
        asked = flat(v.xr[pl.ds(row * 8, 8)])
        neg_exp = jnp.exp(logit_scale * jnp.sum(asked * named, axis=1, keepdims=True))
        v.es[pl.ds(row * 8, 8)] = pack_slots(neg_exp)
        t_e.start_row(row, j == 0)
        rows = (neg_exp * named).reshape(8, SLOTS, EMB).astype(BF16)
        for h in range(2):
            v.ys[h, pl.ds(row * 8, 8)] = rows[:, :, 384 * h : 384 * h + 384]

    loop(0, 4, answer)
    t_qq.start()

    def give(h, j):
        t_y[h].start_row(rem(y + 4 - j, 4), j == 0)

    loop(0, 2, lambda j: give(0, j))

    t_pp.wait_recv()
    pos_exp = jnp.exp(logit_scale * jnp.sum(own_q[...].astype(F32) * v.pp[...].astype(F32), axis=1, keepdims=True))
    v.pos[...] = pack(pos_exp, lead * 6)
    t_pos = Transfer(routes["holder"], lambda i: v.pos, v.posr, s["pos"])
    t_pos.start()

    def total(j, carry):
        row = rem(y + j, 4)
        here = pl.ds(pl.multiple_of(row * QD, QD), QD)
        t_e.wait_row(row)
        parts = three_parts(unpack_slots(v.er[pl.ds(row * 8, 8)]))
        return tuple(carry[half] + mm(v.pick[half, here, :], parts, TN) for half in range(2))

    both = lax.fori_loop(0, 4, total, (jnp.zeros((QD, 128), F32), jnp.zeros((QD, 128), F32)))
    column = jnp.concatenate([jnp.sum(t, axis=1, keepdims=True) for t in both], axis=0)
    v.tot[...] = pack(column)
    t_totl = Transfer(routes["zline"], lambda i: v.tot, v.totl, s["totl"])
    t_toth = Transfer(routes["home"], lambda i: v.tot, v.toth, s["toth"])
    t_totl.start()
    t_toth.start()
    loop(2, 4, lambda j: give(0, j))
    loop(0, 4, lambda j: give(1, j))

    across = routes["xline"]
    t_gx = Transfer(
        across,
        lambda i: v.gs.at[pl.ds(pl.multiple_of(across.item(i) * QD, QD), QD), :],
        v.gx,
        s["gx"],
    )
    t_gx.start()

    t_pos.wait_recv()
    t_totl.wait_recv()
    hard_total = jnp.sum(v.totl[...], axis=0) + jnp.sum(v.posr[...], axis=0)
    inv_hard_tile = 1.0 / jnp.where(lane_of((8, 128)) < 48, hard_total, 1.0)
    inv_hard = [unpack(inv_hard_tile, 24, 24 * half) for half in range(2)]
    inv_parts = [three_parts(inv_hard[half]) for half in range(2)]
    t_inv = PlaneTransfer(v.invs, v.invr, s["inv"], spots)

    def tell(j):
        row = rem(y + j, 4)
        here = pl.ds(pl.multiple_of(row * QD, QD), QD)
        shares = mm(v.pick[0, here, :], inv_parts[0]) + mm(v.pick[1, here, :], inv_parts[1])
        v.invs[pl.ds(row * 8, 8)] = pack_slots(jnp.sum(shares, axis=1, keepdims=True))
        t_inv.start_row(row, j == 0)

    loop(0, 4, tell)
    t_toth.wait_recv()
    own_total = unpack(jnp.sum(v.toth[...], axis=0), 6, lead * 6)
    pos_coef = pos_exp / (pos_exp + own_total) - 2.0
    v.pws[...] = pack(pos_coef)
    t_pw = Transfer(routes["to_passage"], lambda i: v.pws, v.pwr, s["pw"])
    t_pw.start()

    v.hard[...] = jnp.zeros((2, QD, EMB), F32)

    def collect(h):
        lanes = slice(384 * h, 384 * h + 384)

        def gather(j):
            row = rem(y + j, 4)
            here = pl.ds(pl.multiple_of(row * QD, QD), QD)
            t_y[h].wait_row(row)
            rows = v.yr[h, pl.ds(row * 8, 8)].astype(F32).reshape(QD, 384).astype(BF16)
            for half in range(2):
                v.hard[half, :, lanes] += mm(v.pick[half, here, :], rows, TN)

        loop(0, 4, gather)
        for half in range(2):
            own = v.nq[pl.ds(pl.multiple_of(c * 384 + half * QD, QD), QD), lanes]
            mine = own + v.nr[half * QD : half * QD + QD, lanes].astype(F32)
            inv_own = unpack(inv_batch, 24, c * 48 + half * 24)
            mixed = mine * inv_own + v.hard[half, :, lanes] * inv_hard[half]
            v.zs[h, 4 * half : 4 * half + 4] = mixed.astype(BF16).reshape(4, QB, 384)

    home = routes["home"]
    t_z = [
        Transfer(home, lambda i, h=h: v.zs.at[h, home.item(i)], v.zr.at[h], s[name])
        for h, name in enumerate(("z", "z1"))
    ]
    pltpu.make_async_copy(v.nr, v.nr, s["n"][1].at[0]).wait()
    collect(0)
    t_z[0].start()
    collect(1)
    t_z[1].start()

    t_gx.wait_recv()
    v.gy[...] = jnp.sum(v.gx[...].astype(F32), axis=0).astype(BF16)
    along = routes["yline"]
    t_g = Transfer(
        along, lambda i: v.gy.at[pl.ds(pl.multiple_of(along.item(i) * QB, QB), QB), :], v.gr, s["g"]
    )
    t_g.start()

    def weigh(j):
        row = rem(y + 4 - j, 4)
        here = pl.ds(pl.multiple_of(row * QD, QD), QD)
        t_inv.wait_row(row)
        share = unpack_slots(v.es[pl.ds(row * 8, 8)]) * unpack_slots(v.invr[pl.ds(row * 8, 8)])
        v.xw[here, :] = (flat(v.xr[pl.ds(row * 8, 8)]) * share).astype(BF16)

    loop(0, 4, weigh)
    for j in range(2):
        part = mm(v.chosen[:, 256 * j : 256 * j + 256], v.xw[...], TN)
        on[256 * j : 256 * j + 256, :] = (logit_scale * part).astype(BF16)

    for h in range(2):
        t_z[h].wait_recv()
        lanes = slice(384 * h, 384 * h + 384)
        summed = jnp.sum(v.zr[h].astype(F32), axis=0)
        oq[:, lanes] = (logit_scale * (summed + pos_coef * v.pp[:, lanes].astype(F32))).astype(BF16)
    t_pw.wait_recv()
    t_qq.wait_recv()
    t_g.wait_recv()
    summed = jnp.sum(v.gr[...].astype(F32), axis=0)
    coef = unpack(v.pwr[...], 6)
    op[...] = (logit_scale * (summed + coef * v.qq[...].astype(F32))).astype(BF16)

    for t in (t_ids, t_q, t_qq, t_pp, t_p, t_r, t_x, t_pos, t_sums, t_e, *t_y, t_totl, t_toth, t_inv, t_pw, *t_z, t_gx, t_g):
        t.wait_send()
    forward(0).wait_send()
    forward(1).wait_send()
    send_n.wait_send()


def settle_kernel(q, p, n, oq, op, on):
    oq[...] = q[...]
    op[...] = p[...]
    on[...] = n[...]


def shards(query_hidden, passage_hidden, pool_hidden, query_proj, passage_proj, negative_ids):
    scratch = [pltpu.VMEM(shape, dtype) for shape, dtype in SCRATCH.values()]
    for n in PAIRS.values():
        scratch += [pltpu.SemaphoreType.DMA((n,)), pltpu.SemaphoreType.DMA((n,))]
    scratch.append(pltpu.SemaphoreType.DMA((16,)))
    results = pl.pallas_call(
        step_kernel,
        out_shape=[jax.ShapeDtypeStruct((n, EMB), BF16) for n in (QB, QB, 512)],
        in_specs=[pl.BlockSpec(memory_space=pl.ANY)] * 6,
        out_specs=[pl.BlockSpec(memory_space=pltpu.VMEM)] * 3,
        scratch_shapes=scratch,
        compiler_params=pltpu.CompilerParams(
            collective_id=1, has_side_effects=True, vmem_limit_bytes=60 * 1024 * 1024
        ),
        name="contrastive_step",
    )(query_proj, passage_proj, query_hidden, passage_hidden, pool_hidden, negative_ids.T)
    return pl.pallas_call(
        settle_kernel,
        out_shape=[jax.ShapeDtypeStruct((n, EMB), BF16) for n in (QB, QB, 512)],
        in_specs=[pl.BlockSpec(memory_space=pltpu.VMEM)] * 3,
        out_specs=[pl.BlockSpec(memory_space=pltpu.VMEM)] * 3,
        name="settle",
    )(*results)


def solution(mesh):
    placed = (
        P("dp", None),
        P(("tower", "dp"), None),
        P(("tower", "dp"), None),
        P(),
        P(),
        P("dp", None),
    )
    return jax.shard_map(
        shards,
        mesh=mesh,
        in_specs=placed,
        out_specs=(P(("dp", "tower"), None), P(("tower", "dp"), None), P(("tower", "dp"), None)),
        check_vma=False,
    )
```
